512 devices in a mesh: client: 32 (over z, core), param: 16 (over x, y).
Axes of the slice: x: 4, y: 4, z: 16, core: 2. Of those that a mesh axis runs over, the one named last changes fastest.
Arguments:
- inputs: bfloat16 [32, 384, 2304], P('client', None, 'param'), may hold values from -6 to 6
- targets: bfloat16 [32, 384, 2304], P('client', None, 'param'), may hold values from -35 to 35
- norm_gain: float32 [2304], replicated, may hold values from 0.1 to 1.9
- gate_weight: bfloat16 [2304, 4608], P(None, 'param'), may hold values from -0.125 to 0.125
- up_weight: bfloat16 [2304, 4608], P(None, 'param'), may hold values from -0.125 to 0.125
- down_weight: bfloat16 [4608, 2304], P('param'), may hold values from -0.09375 to 0.09375
- neighbours: int32 [32], replicated, may hold values from 9 to 30
Outputs:
- update_gate: float32 [2304, 4608], P('client', 'param')
- update_up: float32 [2304, 4608], P('client', 'param')
- update_down: float32 [2304, 4608], P('client', 'param')
- relative_weight: float32 [32], replicated
The draws below stay inside these ranges and needn't reach their ends.
All inputs are finite; a program needn't handle non-finite values.
Results may differ from the reference program's by a relative error of at most 0.0095.
Values may be sent and summed in bfloat16 or wider, within the bound.
No kernel may reach another device: no remote copies, remote signals or barrier semaphores. Data moves between devices by JAX's collectives and lax.ppermute only.
A program may use at most 64 MiB of HBM per device.

```python
import math
import jax
import jax.numpy as jnp
from jax import lax

D = 2304
FFW = 4608
TOK = 384
CLIENTS = 32
N_CLIENT = 32
N_PARAM = 16


def draw_targets(key, part):
    key_parts = jax.random.split(key, 3)
    client_scale = jnp.exp(jax.random.uniform(key_parts[0], (CLIENTS, 1, 1), jnp.float32, -1.0, 1.0))
    column_scale = jnp.exp(jax.random.uniform(key_parts[1], (1, 1, D), jnp.float32, -1.15, 1.15))
    base_draw = jnp.clip(jax.random.normal(key_parts[2], (CLIENTS, TOK, D), jnp.float32), -4.0, 4.0)
    return (base_draw * client_scale * column_scale).astype(jnp.bfloat16)


def touch_ends(values, key, smallest, high):
    shape = values.shape
    place = [jax.random.randint(jax.random.fold_in(key, axis), (), 0, shape[axis]) for axis in range(len(shape))]
    values = values.at[tuple(place)].set(smallest)
    longest = shape.index(max(shape))
    place[longest] = (place[longest] + 1) % shape[longest]
    return values.at[tuple(place)].set(high)


def steps_of(rng, dims, cuts, low, top_value):
    level = 1.0
    for axis_at, parts in cuts:
        steps = jax.random.uniform(jax.random.fold_in(jax.random.fold_in(rng, 6), axis_at), (parts,), jnp.float32, low / len(cuts), top_value / len(cuts))
        level = level * jnp.repeat(jnp.exp(steps), dims[axis_at] // parts).reshape((-1,) + (1,) * (len(dims) - 1 - axis_at))
    return level


def normal_values(stream_key, extent, scale, most, shards=(), held_as=jnp.bfloat16):
    entries = scale * jax.random.normal(stream_key, extent, jnp.float32)
    if shards:
        entries = entries * steps_of(stream_key, extent, shards, -0.22, 0.18)
    return jnp.clip(entries, -most, most).astype(held_as)


def setup_inputs(seed: int = 0) -> dict:
    streams_of = jax.random.split(jax.random.key(seed), 8)
    return {
        "inputs": normal_values(streams_of[0], (CLIENTS, TOK, D), 1.0, 6.0, ((0, 32), (2, 16))),
        "targets": draw_targets(jax.random.fold_in(streams_of[7], 71), 0),
        "norm_gain": jnp.clip(1.0 + 0.18 * jax.random.normal(streams_of[2], (D,), jnp.float32), 0.1, 1.9),
        "gate_weight": normal_values(streams_of[3], (D, FFW), D ** -0.5, 0.125, ((1, 16),)),
        "up_weight": normal_values(streams_of[4], (D, FFW), D ** -0.5, 0.125, ((1, 16),)),
        "down_weight": normal_values(streams_of[5], (FFW, D), FFW ** -0.5, 0.09375, ((0, 16),)),
        "neighbours": touch_ends(jax.random.randint(streams_of[6], (CLIENTS,), N_CLIENT // 4 + 1, N_CLIENT - 1), jax.random.fold_in(streams_of[6], 1), N_CLIENT // 4 + 1, (N_CLIENT - 1) - 1).astype(jnp.int32),
    }


def gelu_tanh(values):
    return jax.nn.gelu(values, approximate=True)

def rms_normed(gathered, norm_gain):
    widened = gathered.astype(jnp.float32)
    inverse_rms = lax.rsqrt(lax.optimization_barrier(jnp.mean(widened * widened, axis=-1, keepdims=True)) + 1e-06)
    return (widened * inverse_rms * norm_gain.astype(jnp.float32)).astype(jnp.bfloat16)

def krum_weights(gram, neighbours):
    client_count = gram.shape[0]
    diagonal = jnp.diagonal(gram)
    distance = diagonal[:, None] + diagonal[None, :] - 2.0 * gram
    row_index = lax.broadcasted_iota(jnp.int32, (client_count, client_count), 0)
    col_index = lax.broadcasted_iota(jnp.int32, (client_count, client_count), 1)
    distance = jnp.where(row_index == col_index, jnp.asarray(1e+30, gram.dtype), distance)
    ordered = jnp.sort(distance, axis=1)
    scores = lax.optimization_barrier(jnp.sum(jnp.where(col_index < neighbours[:, None], ordered, jnp.zeros_like(ordered)), axis=1))
    scaled = scores / jnp.mean(scores)
    exponent = jnp.exp(-4.0 * scaled)
    return exponent / jnp.sum(exponent)

def reference(inputs, targets, norm_gain, gate_weight, up_weight, down_weight, neighbours):
    factor = 1.0 / math.sqrt(TOK)
    highest = lax.Precision.HIGHEST

    def client_pass(pair_rows):
        client_rows, target_rows = pair_rows
        normed = rms_normed(client_rows, norm_gain)
        gate_value = jnp.dot(normed, gate_weight, preferred_element_type=jnp.float32)
        up_value = jnp.dot(normed, up_weight, preferred_element_type=jnp.float32)
        activated, gelu_back = jax.vjp(gelu_tanh, gate_value)
        hidden = (activated * up_value).astype(jnp.bfloat16)
        out_value = jnp.dot(hidden, down_weight, preferred_element_type=jnp.float32)
        residual = ((out_value - target_rows.astype(jnp.float32)) * factor).astype(jnp.bfloat16)
        back_hidden = lax.dot_general(residual, down_weight, (((1,), (1,)), ((), ())), preferred_element_type=jnp.float32)
        grad_act = gelu_back(back_hidden * up_value)[0]
        back_gate = grad_act.astype(jnp.bfloat16)
        back_up = (back_hidden * activated).astype(jnp.bfloat16)
        return (normed, residual, hidden, back_gate, back_up)
    normed, residual, hidden, back_gate, back_up = lax.map(client_pass, (inputs, targets))
    normed_wide = normed.astype(jnp.float32)
    residual_wide = residual.astype(jnp.float32)
    block_size = FFW // N_PARAM
    offsets = jnp.arange(N_PARAM, dtype=jnp.int32) * block_size

    def deltas_at(offset):

        def columns(array):
            return lax.dynamic_slice_in_dim(array, offset, block_size, 2).astype(jnp.float32)
        gate_delta = (-jnp.einsum('ctd,ctf->cdf', normed_wide, columns(back_gate), precision=highest)).astype(jnp.bfloat16)
        up_delta = (-jnp.einsum('ctd,ctf->cdf', normed_wide, columns(back_up), precision=highest)).astype(jnp.bfloat16)
        down_delta = (-jnp.einsum('ctd,ctf->cdf', residual_wide, columns(hidden), precision=highest)).astype(jnp.bfloat16)
        return (gate_delta, up_delta, down_delta)

    def gram_step(running, offset):
        for delta_block in deltas_at(offset):
            widened = delta_block.astype(jnp.float32)
            running = running + jnp.einsum('cdf,edf->ce', widened, widened, precision=highest)
        return (running, None)
    gram, _ = lax.scan(gram_step, jnp.zeros((N_CLIENT, N_CLIENT), jnp.float32), offsets)
    weights = krum_weights(gram, neighbours)

    def update_step(offset):
        return tuple((lax.optimization_barrier(jnp.sum(weights[:, None, None] * delta_block.astype(jnp.float32), axis=0)) for delta_block in deltas_at(offset)))
    blocks = lax.map(update_step, offsets)

    def assemble(stacked):
        return jnp.transpose(stacked, (1, 0, 2)).reshape(D, FFW)
    return (assemble(blocks[0]), assemble(blocks[1]), assemble(blocks[2]), N_CLIENT * weights)
```

```python
import math

import jax
import jax.numpy as jnp
from jax import lax
from jax.experimental import pallas as pl
from jax.experimental.pallas import tpu as pltpu
from jax.sharding import Mesh, PartitionSpec as P

XY = ("x", "y")
ZC = ("z", "core")


def gelu_tanh(values):
    return jax.nn.gelu(values, approximate=True)


def exchange(blocks, axes):
    return lax.all_to_all(blocks, axes, split_axis=0, concat_axis=0, tiled=True)


def gather_rows(shard, axes, count):
    copies = jnp.broadcast_to(shard[None], (count,) + shard.shape)
    return exchange(copies, axes).reshape((count * shard.shape[0],) + shard.shape[1:])


def contract(left, right, left_dim, right_dim):
    return lax.dot_general(
        left, right, (((left_dim,), (right_dim,)), ((), ())), preferred_element_type=jnp.float32
    )


def krum_weights(gram, neighbours):
    client_count = gram.shape[0]
    row_index = lax.broadcasted_iota(jnp.int32, (client_count, client_count), 0)
    col_index = lax.broadcasted_iota(jnp.int32, (client_count, client_count), 1)
    diagonal = jnp.sum(jnp.where(row_index == col_index, gram, 0.0), axis=1)
    distance = diagonal[:, None] + diagonal[None, :] - 2.0 * gram
    distance = jnp.where(row_index == col_index, jnp.asarray(1e30, gram.dtype), distance)
    ordered = jnp.sort(distance, axis=1)
    scores = jnp.sum(
        jnp.where(col_index < neighbours[:, None], ordered, jnp.zeros_like(ordered)), axis=1
    )
    scaled = scores / jnp.mean(scores)
    exponent = jnp.exp(-4.0 * scaled)
    return exponent / jnp.sum(exponent)


def gram_kernel(block_ref, gram_ref, total_ref):
    clients, rows, columns = block_ref.shape
    step = 8
    total_ref[...] = jnp.zeros_like(total_ref)

    @pl.loop(0, rows // step)
    def _(index):
        start = pl.multiple_of(index * step, step)
        tile = block_ref[:, pl.ds(start, step), :].reshape(clients * step, columns)
        total_ref[...] += contract(tile, tile, 1, 1)

    size = clients * step
    row_index = lax.broadcasted_iota(jnp.int32, (size, size), 0)
    col_index = lax.broadcasted_iota(jnp.int32, (size, size), 1)
    kept = jnp.where(row_index % step == col_index % step, total_ref[...], 0.0)
    pick_client = lax.broadcasted_iota(jnp.int32, (clients, size), 0)
    pick_row = lax.broadcasted_iota(jnp.int32, (clients, size), 1)
    pick = (pick_row // step == pick_client).astype(jnp.float32)
    half = lax.dot_general(
        pick, kept, (((1,), (0,)), ((), ())),
        precision=lax.Precision.HIGHEST, preferred_element_type=jnp.float32,
    )
    gram_ref[...] = lax.dot_general(
        half, pick, (((1,), (1,)), ((), ())),
        precision=lax.Precision.HIGHEST, preferred_element_type=jnp.float32,
    )


def pair_products(exchanged):
    clients, rows, columns = exchanged.shape
    return pl.pallas_call(
        gram_kernel,
        out_shape=jax.ShapeDtypeStruct((clients, clients), jnp.float32),
        in_specs=[pl.BlockSpec(memory_space=pltpu.VMEM)],
        out_specs=pl.BlockSpec(memory_space=pltpu.VMEM),
        scratch_shapes=[pltpu.VMEM((clients * 8, clients * 8), jnp.float32)],
        cost_estimate=pl.CostEstimate(
            flops=2 * rows * clients * clients * 8 * columns,
            bytes_accessed=2 * clients * rows * columns,
            transcendentals=0,
        ),
        name="pair_products",
    )(exchanged)


def sum_over(values, axes, count):
    copies = jnp.broadcast_to(values[None], (count,) + values.shape)
    return jnp.sum(exchange(copies, axes), axis=0)


def on_device(inputs, targets, norm_gain, gate_weight, up_weight, down_weight, neighbours):
    token_count = inputs.shape[1]
    param_count = lax.axis_size(XY)
    client_count = lax.axis_size(ZC)
    z_count = lax.axis_size("z")
    factor = 1.0 / math.sqrt(token_count)
    features = param_count * inputs.shape[2]
    hidden_units = gate_weight.shape[1]

    gathered = gather_rows(inputs[0].T, XY, param_count).astype(jnp.float32)
    inverse_rms = lax.rsqrt(jnp.mean(gathered * gathered, axis=0, keepdims=True) + 1e-06)
    normed = (gathered * inverse_rms * norm_gain[:, None]).astype(jnp.bfloat16)
    gate_value = contract(gate_weight, normed, 0, 0)
    up_value = contract(up_weight, normed, 0, 0)
    activated, gelu_back = jax.vjp(gelu_tanh, gate_value)
    hidden = (activated * up_value).astype(jnp.bfloat16)
    partial_out = contract(down_weight, hidden, 0, 0).astype(jnp.bfloat16)
    parts = exchange(partial_out.reshape(param_count, features // param_count, token_count), XY)
    summed = jnp.sum(parts.astype(jnp.float32), axis=0)
    own_residual = ((summed - targets[0].T.astype(jnp.float32)) * factor).astype(jnp.bfloat16)
    residual = gather_rows(own_residual, XY, param_count)
    back_hidden = contract(down_weight, residual, 1, 0)
    back_gate = gelu_back(back_hidden * up_value)[0].astype(jnp.bfloat16)
    back_up = (back_hidden * activated).astype(jnp.bfloat16)

    width = -(-3 * hidden_units // 128) * 128
    zeros = jnp.zeros((hidden_units, token_count), jnp.bfloat16)
    rest = jnp.zeros((width - 3 * hidden_units, 2 * token_count), jnp.bfloat16)
    left = jnp.concatenate([normed, residual], axis=1)
    right = jnp.concatenate(
        [
            jnp.concatenate([back_gate, zeros], axis=1),
            jnp.concatenate([back_up, zeros], axis=1),
            jnp.concatenate([zeros, hidden], axis=1),
            rest,
        ],
        axis=0,
    )
    deltas = (-contract(left, right, 1, 1)).astype(jnp.bfloat16)
    owned = exchange(deltas.reshape(client_count, features // client_count, width), ZC)

    gram = pair_products(owned).reshape(8, -1)
    gram = lax.psum(gram, "core")
    gram = sum_over(gram, XY, param_count)
    gram = sum_over(gram, "z", z_count).reshape(client_count, client_count)
    weights = krum_weights(gram, neighbours)
    update = jnp.sum(weights[:, None, None] * owned.astype(jnp.float32), axis=0)
    return (
        update[:, :hidden_units],
        update[:, hidden_units : 2 * hidden_units],
        update[:, 2 * hidden_units : 3 * hidden_units],
        client_count * weights,
    )


def solution(mesh):
    torus = Mesh(mesh.devices.reshape(16, 2, 4, 4), ("z", "core", "x", "y"))
    in_specs = (
        P(ZC, None, XY),
        P(ZC, None, XY),
        P(),
        P(None, XY),
        P(None, XY),
        P(XY, None),
        P(),
    )
    out_specs = (P(ZC, XY), P(ZC, XY), P(ZC, XY), P())
    return jax.shard_map(
        on_device, mesh=torus, in_specs=in_specs, out_specs=out_specs, check_vma=False
    )
```

```python
import math

import jax
import jax.numpy as jnp
from jax import lax
from jax.experimental import pallas as pl
from jax.experimental.pallas import tpu as pltpu
from jax.sharding import Mesh, PartitionSpec as P


XY = ("x", "y")
ZC = ("z", "core")


def gelu_tanh(values):
    return jax.nn.gelu(values, approximate=True)


def exchange(blocks, axes):
    return lax.all_to_all(blocks, axes, split_axis=0, concat_axis=0, tiled=True)


def gather_rows(shard, axes, count):
    copies = jnp.broadcast_to(shard[None], (count,) + shard.shape)
    return exchange(copies, axes).reshape((count * shard.shape[0],) + shard.shape[1:])


def contract(left, right, left_dim, right_dim):
    return lax.dot_general(
        left, right, (((left_dim,), (right_dim,)), ((), ())), preferred_element_type=jnp.float32
    )


def krum_weights(gram, neighbours):
    client_count = gram.shape[0]
    row_index = lax.broadcasted_iota(jnp.int32, (client_count, client_count), 0)
    col_index = lax.broadcasted_iota(jnp.int32, (client_count, client_count), 1)
    diagonal = jnp.sum(jnp.where(row_index == col_index, gram, 0.0), axis=1)
    distance = diagonal[:, None] + diagonal[None, :] - 2.0 * gram
    distance = jnp.where(row_index == col_index, jnp.asarray(1e30, gram.dtype), distance)
    ordered = jnp.sort(distance, axis=1)
    scores = jnp.sum(
        jnp.where(col_index < neighbours[:, None], ordered, jnp.zeros_like(ordered)), axis=1
    )
    scaled = scores / jnp.mean(scores)
    exponent = jnp.exp(-4.0 * scaled)
    return exponent / jnp.sum(exponent)


def gram_kernel(block_ref, gram_ref, total_ref):
    clients, rows, columns = block_ref.shape
    step = 8
    total_ref[...] = jnp.zeros_like(total_ref)

    @pl.loop(0, rows // step)
    def _(index):
        start = pl.multiple_of(index * step, step)
        tile = block_ref[:, pl.ds(start, step), :].reshape(clients * step, columns)
        total_ref[...] += contract(tile, tile, 1, 1)

    size = clients * step
    row_index = lax.broadcasted_iota(jnp.int32, (size, size), 0)
    col_index = lax.broadcasted_iota(jnp.int32, (size, size), 1)
    kept = jnp.where(row_index % step == col_index % step, total_ref[...], 0.0)
    pick_client = lax.broadcasted_iota(jnp.int32, (clients, size), 0)
    pick_row = lax.broadcasted_iota(jnp.int32, (clients, size), 1)
    pick = (pick_row // step == pick_client).astype(jnp.float32)
    half = lax.dot_general(
        pick, kept, (((1,), (0,)), ((), ())),
        precision=lax.Precision.HIGHEST, preferred_element_type=jnp.float32,
    )
    gram_ref[...] = lax.dot_general(
        half, pick, (((1,), (1,)), ((), ())),
        precision=lax.Precision.HIGHEST, preferred_element_type=jnp.float32,
    )


def pair_products(exchanged):
    clients, rows, columns = exchanged.shape
    return pl.pallas_call(
        gram_kernel,
        out_shape=jax.ShapeDtypeStruct((clients, clients), jnp.float32),
        in_specs=[pl.BlockSpec(memory_space=pltpu.VMEM)],
        out_specs=pl.BlockSpec(memory_space=pltpu.VMEM),
        scratch_shapes=[pltpu.VMEM((clients * 8, clients * 8), jnp.float32)],
        cost_estimate=pl.CostEstimate(
            flops=2 * rows * clients * clients * 8 * columns,
            bytes_accessed=2 * clients * rows * columns,
            transcendentals=0,
        ),
        name="pair_products",
    )(exchanged)


def sum_over(values, axes, count):
    copies = jnp.broadcast_to(values[None], (count,) + values.shape)
    return jnp.sum(exchange(copies, axes), axis=0)


def rms_normed(raw, norm_gain):
    widened = raw.astype(jnp.float32)
    inverse_rms = lax.rsqrt(jnp.mean(widened * widened, axis=0, keepdims=True) + 1e-06)
    return (widened * inverse_rms * norm_gain[:, None]).astype(jnp.bfloat16)


def swap_blocks(shard, z_count, core_count):
    pairs = [
        ((z * core_count + core) * z_count + p, (p * core_count + core) * z_count + z)
        for z in range(z_count)
        for core in range(core_count)
        for p in range(z_count)
    ]
    return lax.ppermute(shard, ZC + XY, pairs)


def on_device(inputs, targets, norm_gain, gate_weight, up_weight, down_weight, neighbours):
    token_count = inputs.shape[1]
    param_count = lax.axis_size(XY)
    z_count = lax.axis_size("z")
    core_count = lax.axis_size("core")
    client_count = z_count * core_count
    factor = 1.0 / math.sqrt(token_count)
    features = param_count * inputs.shape[2]
    slice_rows = features // client_count
    hidden_units = gate_weight.shape[1]

    own_inputs = inputs[0].T
    met_inputs = swap_blocks(own_inputs, z_count, core_count)
    met_inputs = lax.all_gather(met_inputs, "z", axis=0, tiled=True)
    gathered = gather_rows(own_inputs, XY, param_count)
    normed = rms_normed(gathered, norm_gain)
    gate_value = contract(gate_weight, normed, 0, 0)
    up_value = contract(up_weight, normed, 0, 0)
    activated, gelu_back = jax.vjp(gelu_tanh, gate_value)
    hidden = (activated * up_value).astype(jnp.bfloat16)
    partial_out = contract(down_weight, hidden, 0, 0).astype(jnp.bfloat16)
    parts = exchange(
        partial_out.reshape(param_count, features // param_count, token_count), XY
    )
    summed = jnp.sum(parts.astype(jnp.float32), axis=0)
    own_residual = ((summed - targets[0].T.astype(jnp.float32)) * factor).astype(jnp.bfloat16)
    met_residual = swap_blocks(own_residual, z_count, core_count)
    met_residual = lax.all_gather(met_residual, "z", axis=0, tiled=True)
    residual = gather_rows(own_residual, XY, param_count)
    back_hidden = contract(down_weight, residual, 1, 0)
    back_gate = gelu_back(back_hidden * up_value)[0].astype(jnp.bfloat16)
    back_up = (back_hidden * activated).astype(jnp.bfloat16)

    height = -(-3 * hidden_units // (8 * z_count)) * 8
    rest = jnp.zeros((height * z_count - 3 * hidden_units, token_count), jnp.bfloat16)
    rows = jnp.concatenate([back_gate, back_up, hidden, rest], axis=0)
    rows, met_inputs = lax.optimization_barrier((rows, met_inputs))
    rows = exchange(rows.reshape(z_count, height, token_count), "z")
    rows = exchange(rows, XY)
    place = lax.axis_index("z") * height + lax.broadcasted_iota(jnp.int32, (1, height, 1), 1)
    of_down = place >= 2 * hidden_units
    left = jnp.concatenate(
        [jnp.where(of_down, 0, rows), jnp.where(of_down, rows, 0)], axis=2
    ).reshape(param_count * height, 2 * token_count)
    right = jnp.concatenate([rms_normed(met_inputs, norm_gain), met_residual], axis=1)
    right = right.reshape(z_count, core_count, slice_rows, 2 * token_count)
    half = z_count * slice_rows
    deltas = [
        (-contract(left, right[:, core].reshape(half, 2 * token_count), 1, 1))
        .astype(jnp.bfloat16)
        .reshape(param_count, height, half)
        for core in range(core_count)
    ]
    owned = exchange(jnp.concatenate(deltas, axis=0), ("core",) + XY)

    gram = pair_products(owned).reshape(8, -1)
    gram = sum_over(gram, ("core",) + XY, core_count * param_count)
    gram = sum_over(gram, "z", z_count).reshape(client_count, client_count)
    weights = krum_weights(gram, neighbours.reshape(z_count, core_count).T.reshape(-1))
    update = jnp.sum(weights[:, None, None] * owned.astype(jnp.float32), axis=0)
    update = update.astype(jnp.bfloat16).reshape(height, z_count, slice_rows).swapaxes(0, 1)
    update = exchange(update, "z").reshape(z_count * height, slice_rows).T.astype(jnp.float32)
    return (
        update[:, :hidden_units],
        update[:, hidden_units : 2 * hidden_units],
        update[:, 2 * hidden_units : 3 * hidden_units],
        client_count * weights.reshape(core_count, z_count).T.reshape(-1),
    )


def solution(mesh):
    torus = Mesh(mesh.devices.reshape(16, 2, 4, 4), ("z", "core", "x", "y"))
    in_specs = (
        P(ZC, None, XY),
        P(ZC, None, XY),
        P(),
        P(None, XY),
        P(None, XY),
        P(XY, None),
        P(),
    )
    out_specs = (P(ZC, XY), P(ZC, XY), P(ZC, XY), P())
    return jax.shard_map(
        on_device, mesh=torus, in_specs=in_specs, out_specs=out_specs, check_vma=False
    )
```

```python
import math

import jax
import jax.numpy as jnp
from jax import lax
from jax.experimental import pallas as pl
from jax.experimental.pallas import tpu as pltpu
from jax.sharding import Mesh, PartitionSpec as P

XY = ("x", "y")
ZC = ("z", "core")


def exchange(blocks, axes):
    return lax.all_to_all(blocks, axes, split_axis=0, concat_axis=0, tiled=True)


def gather_rows(shard, axes, count):
    copies = jnp.broadcast_to(shard[None], (count,) + shard.shape)
    return exchange(copies, axes).reshape((count * shard.shape[0],) + shard.shape[1:])


def contract(left, right, left_dim, right_dim):
    return lax.dot_general(
        left, right, (((left_dim,), (right_dim,)), ((), ())), preferred_element_type=jnp.float32
    )


def gelu_parts(values):
    scale = math.sqrt(2.0 / math.pi)
    square = values * values
    bend = jnp.tanh(scale * (values + 0.044715 * (square * values)))
    slope = 0.5 * (1.0 + bend) + (0.5 * values) * (1.0 - bend * bend) * (
        scale * (1.0 + (3.0 * 0.044715) * square)
    )
    return 0.5 * values * (1.0 + bend), slope


def forward_kernel(
    normed_ref, gate_ref, up_ref, down_ref,
    out_ref, hidden_ref, activated_ref, slope_ref,
    gate_total, up_total,
):
    step = pl.program_id(0)
    half = pl.num_programs(0) // 2

    @pl.when(step == 0)
    def _():
        gate_total[...] = jnp.zeros_like(gate_total)
        up_total[...] = jnp.zeros_like(up_total)

    @pl.when(step < half)
    def _():
        rows = normed_ref[...]
        gate_total[...] += contract(gate_ref[...], rows, 1, 0)
        up_total[...] += contract(up_ref[...], rows, 1, 0)

    @pl.when(step == half - 1)
    def _():
        activated, slope = gelu_parts(gate_total[...])
        up_value = up_total[...]
        activated_ref[...] = activated
        slope_ref[...] = slope * up_value
        hidden_ref[...] = (activated * up_value).astype(hidden_ref.dtype)

    @pl.when(step >= half)
    def _():
        out_ref[...] = contract(down_ref[...], hidden_ref[...], 0, 0).astype(out_ref.dtype)


def forward(normed, gate_weight, up_weight, down_weight):
    features, tokens = normed.shape
    units = down_weight.shape[0]
    chunks = 3
    rows = features // chunks
    early = lambda step: jnp.minimum(step, chunks - 1)
    late = lambda step: jnp.maximum(step - chunks, 0)
    whole = pl.BlockSpec((units, tokens), lambda step: (0, 0))
    return pl.pallas_call(
        forward_kernel,
        grid=(2 * chunks,),
        in_specs=[
            pl.BlockSpec((rows, tokens), lambda step: (early(step), 0)),
            pl.BlockSpec((units, rows), lambda step: (0, early(step))),
            pl.BlockSpec((units, rows), lambda step: (0, early(step))),
            pl.BlockSpec((units, rows), lambda step: (0, late(step))),
        ],
        out_specs=[pl.BlockSpec((rows, tokens), lambda step: (late(step), 0)), whole, whole, whole],
        out_shape=[
            jax.ShapeDtypeStruct((features, tokens), jnp.bfloat16),
            jax.ShapeDtypeStruct((units, tokens), jnp.bfloat16),
            jax.ShapeDtypeStruct((units, tokens), jnp.float32),
            jax.ShapeDtypeStruct((units, tokens), jnp.float32),
        ],
        scratch_shapes=[pltpu.VMEM((units, tokens), jnp.float32)] * 2,
        cost_estimate=pl.CostEstimate(
            flops=6 * features * tokens * units,
            bytes_accessed=2 * features * (3 * units + 2 * tokens) + 10 * units * tokens,
            transcendentals=units * tokens,
        ),
        name="forward",
    )(normed, gate_weight.T, up_weight.T, down_weight)


def exact_dot(left, right, left_dim, right_dim):
    return lax.dot_general(
        left, right, (((left_dim,), (right_dim,)), ((), ())),
        precision=lax.Precision.HIGHEST, preferred_element_type=jnp.float32,
    )


def lane_place(index, size, lanes):
    row = lax.broadcasted_iota(jnp.int32, (size, lanes), 0)
    column = lax.broadcasted_iota(jnp.int32, (size, lanes), 1)
    return (column == row + index * size).astype(jnp.float32)


def gram_kernel(core_ref, own_ref, other_ref, copies_ref, total_ref):
    step = pl.program_id(0)
    half, _, rows, columns = own_ref.shape
    clients, tall = 2 * half, 8
    size = clients * tall

    @pl.when(step == 0)
    def _():
        total_ref[...] = jnp.zeros_like(total_ref)

    for start in range(0, rows, tall):
        tile = jnp.concatenate(
            [own_ref[:, 0, start : start + tall, :], other_ref[:, start : start + tall, :]], axis=0
        ).reshape(size, columns)
        total_ref[...] += contract(tile, tile, 1, 1)

    @pl.when(step == pl.num_programs(0) - 1)
    def _():
        row_index = lax.broadcasted_iota(jnp.int32, (size, size), 0)
        col_index = lax.broadcasted_iota(jnp.int32, (size, size), 1)
        kept = jnp.where(row_index % tall == col_index % tall, total_ref[...], 0.0)
        pick_client = lax.broadcasted_iota(jnp.int32, (clients, size), 0)
        pick_row = lax.broadcasted_iota(jnp.int32, (clients, size), 1) // tall
        pick_row = (pick_row + half * core_ref[0]) % clients
        pick = (pick_row == pick_client).astype(jnp.float32)
        gram = exact_dot(exact_dot(pick, kept, 1, 0), pick, 1, 1)
        packed = jnp.zeros(copies_ref.shape[1:], jnp.float32)
        for index in range(clients // tall):
            packed += exact_dot(
                gram[index * tall : (index + 1) * tall],
                lane_place(index, clients, copies_ref.shape[2]), 1, 0,
            )
        copies_ref[...] = jnp.broadcast_to(packed[None], copies_ref.shape)


def pair_products(core, own, other, copies):
    half, _, rows, columns = own.shape
    chunks = 3
    return pl.pallas_call(
        gram_kernel,
        grid_spec=pltpu.PrefetchScalarGridSpec(
            num_scalar_prefetch=1,
            grid=(chunks,),
            in_specs=[
                pl.BlockSpec(
                    (half, 1, rows // chunks, columns), lambda step, core_ref: (0, core_ref[0], step, 0)
                ),
                pl.BlockSpec((half, rows // chunks, columns), lambda step, core_ref: (0, step, 0)),
            ],
            out_specs=pl.BlockSpec((copies, 8, 128), lambda step, core_ref: (0, 0, 0)),
            scratch_shapes=[pltpu.VMEM((half * 16, half * 16), jnp.float32)],
        ),
        out_shape=jax.ShapeDtypeStruct((copies, 8, 128), jnp.float32),
        cost_estimate=pl.CostEstimate(
            flops=2 * rows * 4 * half * half * 8 * columns,
            bytes_accessed=4 * half * rows * columns,
            transcendentals=0,
        ),
        name="pair_products",
    )(core, own, other)


def finish_kernel(
    core_ref, parts_ref, neighbours_ref, own_ref, other_ref,
    gate_ref, up_ref, down_ref, relative_ref, weight_ref,
):
    step = pl.program_id(0)
    half, _, rows, _ = own_ref.shape
    clients, tall = 2 * half, 8
    units = gate_ref.shape[1]

    @pl.when(step == 0)
    def _():
        packed = jnp.sum(parts_ref[...], axis=0)
        gram = jnp.concatenate(
            [
                exact_dot(packed, lane_place(index, clients, packed.shape[1]), 1, 1)
                for index in range(clients // tall)
            ],
            axis=0,
        )
        row_index = lax.broadcasted_iota(jnp.int32, (clients, clients), 0)
        col_index = lax.broadcasted_iota(jnp.int32, (clients, clients), 1)
        same = row_index == col_index
        diagonal = jnp.where(same, gram, 0.0)
        distance = (
            jnp.sum(diagonal, axis=1, keepdims=True)
            + jnp.sum(diagonal, axis=0, keepdims=True)
            - 2.0 * gram
        )
        distance = jnp.where(same, 1e30, distance)
        rank = jnp.zeros((clients, clients), jnp.float32)
        for index in range(clients):
            rival = distance[:, index : index + 1]
            ahead = (rival < distance) | ((rival == distance) & (index < col_index))
            rank += jnp.where(ahead, 1.0, 0.0)
        count = jnp.sum(
            jnp.where(same, neighbours_ref[...].astype(jnp.float32), 0.0), axis=1, keepdims=True
        )
        scores = jnp.sum(jnp.where(rank < count, distance, 0.0), axis=1, keepdims=True)
        mean = jnp.sum(scores, axis=0, keepdims=True) / clients
        exponent = jnp.exp(-4.0 * (scores / mean))
        weights = exponent / jnp.sum(exponent, axis=0, keepdims=True)
        relative_ref[...] = clients * jnp.sum(
            jnp.where(same, weights, 0.0), axis=0, keepdims=True
        )
        weight_ref[...] = jnp.broadcast_to(weights, weight_ref.shape)

    core = core_ref[0]
    own_weight = weight_ref[pl.ds(pl.multiple_of(core * half, half), half), :]
    other_weight = weight_ref[pl.ds(pl.multiple_of((1 - core) * half, half), half), :]
    for start in range(0, rows, tall):
        total = jnp.zeros((tall, own_ref.shape[3]), jnp.float32)
        for index in range(half):
            total += own_weight[index : index + 1, :1] * own_ref[
                index, 0, start : start + tall, :
            ].astype(jnp.float32)
            total += other_weight[index : index + 1, :1] * other_ref[
                index, start : start + tall, :
            ].astype(jnp.float32)
        gate_ref[start : start + tall, :] = total[:, :units]
        up_ref[start : start + tall, :] = total[:, units : 2 * units]
        down_ref[start : start + tall, :] = total[:, 2 * units : 3 * units]


def finish(core, parts, neighbours, own, other, units):
    half, _, rows, columns = own.shape
    chunks = 3
    tall = rows // chunks
    block = pl.BlockSpec((tall, units), lambda step, core_ref: (step, 0))
    return pl.pallas_call(
        finish_kernel,
        grid_spec=pltpu.PrefetchScalarGridSpec(
            num_scalar_prefetch=1,
            grid=(chunks,),
            in_specs=[
                pl.BlockSpec(parts.shape, lambda step, core_ref: (0, 0, 0)),
                pl.BlockSpec(neighbours.shape, lambda step, core_ref: (0, 0)),
                pl.BlockSpec(
                    (half, 1, tall, columns), lambda step, core_ref: (0, core_ref[0], step, 0)
                ),
                pl.BlockSpec((half, tall, columns), lambda step, core_ref: (0, step, 0)),
            ],
            out_specs=[
                block, block, block, pl.BlockSpec((1, 2 * half), lambda step, core_ref: (0, 0))
            ],
            scratch_shapes=[pltpu.VMEM((2 * half, 128), jnp.float32)],
        ),
        out_shape=[jax.ShapeDtypeStruct((rows, units), jnp.float32)] * 3
        + [jax.ShapeDtypeStruct((1, 2 * half), jnp.float32)],
        cost_estimate=pl.CostEstimate(
            flops=4 * half * rows * columns,
            bytes_accessed=4 * half * rows * columns + 12 * rows * units,
            transcendentals=2 * half,
        ),
        name="finish",
    )(core, parts, neighbours, own, other)


def on_device(inputs, targets, norm_gain, gate_weight, up_weight, down_weight, neighbours):
    token_count = inputs.shape[1]
    param_count = lax.axis_size(XY)
    z_count = lax.axis_size("z")
    core_count = lax.axis_size("core")
    client_count = z_count * core_count
    factor = 1.0 / math.sqrt(token_count)
    features = param_count * inputs.shape[2]
    hidden_units = gate_weight.shape[1]
    core = lax.axis_index("core")

    gathered = gather_rows(inputs[0].T, XY, param_count).astype(jnp.float32)
    inverse_rms = lax.rsqrt(jnp.mean(gathered * gathered, axis=0, keepdims=True) + 1e-06)
    normed = (gathered * inverse_rms * norm_gain[:, None]).astype(jnp.bfloat16)
    partial_out, hidden, activated, slope = forward(normed, gate_weight, up_weight, down_weight)
    parts = exchange(partial_out.reshape(param_count, features // param_count, token_count), XY)
    summed = jnp.sum(parts.astype(jnp.float32), axis=0)
    own_residual = ((summed - targets[0].T.astype(jnp.float32)) * factor).astype(jnp.bfloat16)
    residual = gather_rows(own_residual, XY, param_count)
    back_hidden = contract(down_weight, residual, 1, 0)
    back_gate = (back_hidden * slope).astype(jnp.bfloat16)
    back_up = (back_hidden * activated).astype(jnp.bfloat16)

    width = -(-3 * hidden_units // 128) * 128
    zeros = jnp.zeros((hidden_units, token_count), jnp.bfloat16)
    rest = jnp.zeros((width - 3 * hidden_units, 2 * token_count), jnp.bfloat16)
    left = jnp.concatenate([normed, residual], axis=1)
    right = jnp.concatenate(
        [
            jnp.concatenate([back_gate, zeros], axis=1),
            jnp.concatenate([back_up, zeros], axis=1),
            jnp.concatenate([zeros, hidden], axis=1),
            rest,
        ],
        axis=0,
    )
    deltas = (-contract(left, right, 1, 1)).astype(jnp.bfloat16)
    met = exchange(deltas.reshape(z_count, features // z_count, width), "z")
    met = met.reshape(z_count, core_count, features // client_count, width)
    other = lax.dynamic_index_in_dim(met, 1 - core, axis=1, keepdims=False)
    other = lax.ppermute(other, "core", [(0, 1), (1, 0)])

    core = core.reshape(1)
    gram = pair_products(core, met, other, core_count * param_count)
    gram = jnp.sum(exchange(gram, ("core",) + XY), axis=0)
    gram = exchange(jnp.broadcast_to(gram[None], (z_count,) + gram.shape), "z")
    order = neighbours.reshape(z_count, core_count).T.reshape(1, -1)
    update_gate, update_up, update_down, relative = finish(
        core, gram, order, met, other, hidden_units
    )
    return (
        update_gate,
        update_up,
        update_down,
        relative.reshape(core_count, z_count).T.reshape(-1),
    )


def solution(mesh):
    torus = Mesh(mesh.devices.reshape(16, 2, 4, 4), ("z", "core", "x", "y"))
    in_specs = (
        P(ZC, None, XY),
        P(ZC, None, XY),
        P(),
        P(None, XY),
        P(None, XY),
        P(XY, None),
        P(),
    )
    out_specs = (P(ZC, XY), P(ZC, XY), P(ZC, XY), P())
    return jax.shard_map(
        on_device, mesh=torus, in_specs=in_specs, out_specs=out_specs, check_vma=False
    )
```

```python
import math

import jax
import jax.numpy as jnp
from jax import lax
from jax.experimental import pallas as pl
from jax.experimental.pallas import tpu as pltpu
from jax.sharding import Mesh, PartitionSpec as P


XY = ("x", "y")
ZC = ("z", "core")


def gelu_tanh(values):
    return jax.nn.gelu(values, approximate=True)


def exchange(blocks, axes):
    return lax.all_to_all(blocks, axes, split_axis=0, concat_axis=0, tiled=True)


def gather_rows(shard, axes, count):
    copies = jnp.broadcast_to(shard[None], (count,) + shard.shape)
    return exchange(copies, axes).reshape((count * shard.shape[0],) + shard.shape[1:])


def contract(left, right, left_dim, right_dim):
    return lax.dot_general(
        left, right, (((left_dim,), (right_dim,)), ((), ())), preferred_element_type=jnp.float32
    )


def krum_weights(gram, neighbours):
    client_count = gram.shape[0]
    row_index = lax.broadcasted_iota(jnp.int32, (client_count, client_count), 0)
    col_index = lax.broadcasted_iota(jnp.int32, (client_count, client_count), 1)
    diagonal = jnp.sum(jnp.where(row_index == col_index, gram, 0.0), axis=1)
    distance = diagonal[:, None] + diagonal[None, :] - 2.0 * gram
    distance = jnp.where(row_index == col_index, jnp.asarray(1e30, gram.dtype), distance)
    ordered = jnp.sort(distance, axis=1)
    scores = jnp.sum(
        jnp.where(col_index < neighbours[:, None], ordered, jnp.zeros_like(ordered)), axis=1
    )
    scaled = scores / jnp.mean(scores)
    exponent = jnp.exp(-4.0 * scaled)
    return exponent / jnp.sum(exponent)


def gram_kernel(block_ref, gram_ref, total_ref):
    clients, rows, columns = block_ref.shape
    step = 8
    total_ref[...] = jnp.zeros_like(total_ref)

    @pl.loop(0, rows // step)
    def _(index):
        start = pl.multiple_of(index * step, step)
        tile = block_ref[:, pl.ds(start, step), :].reshape(clients * step, columns)
        total_ref[...] += contract(tile, tile, 1, 1)

    size = clients * step
    row_index = lax.broadcasted_iota(jnp.int32, (size, size), 0)
    col_index = lax.broadcasted_iota(jnp.int32, (size, size), 1)
    kept = jnp.where(row_index % step == col_index % step, total_ref[...], 0.0)
    pick_client = lax.broadcasted_iota(jnp.int32, (clients, size), 0)
    pick_row = lax.broadcasted_iota(jnp.int32, (clients, size), 1)
    pick = (pick_row // step == pick_client).astype(jnp.float32)
    half = lax.dot_general(
        pick, kept, (((1,), (0,)), ((), ())),
        precision=lax.Precision.HIGHEST, preferred_element_type=jnp.float32,
    )
    gram_ref[...] = lax.dot_general(
        half, pick, (((1,), (1,)), ((), ())),
        precision=lax.Precision.HIGHEST, preferred_element_type=jnp.float32,
    )


def pair_products(exchanged):
    clients, rows, columns = exchanged.shape
    return pl.pallas_call(
        gram_kernel,
        out_shape=jax.ShapeDtypeStruct((clients, clients), jnp.float32),
        in_specs=[pl.BlockSpec(memory_space=pltpu.VMEM)],
        out_specs=pl.BlockSpec(memory_space=pltpu.VMEM),
        scratch_shapes=[pltpu.VMEM((clients * 8, clients * 8), jnp.float32)],
        cost_estimate=pl.CostEstimate(
            flops=2 * rows * clients * clients * 8 * columns,
            bytes_accessed=2 * clients * rows * columns,
            transcendentals=0,
        ),
        name="pair_products",
    )(exchanged)


def sum_over(values, axes, count):
    copies = jnp.broadcast_to(values[None], (count,) + values.shape)
    return jnp.sum(exchange(copies, axes), axis=0)


def rms_normed(raw, norm_gain):
    widened = raw.astype(jnp.float32)
    inverse_rms = lax.rsqrt(jnp.mean(widened * widened, axis=0, keepdims=True) + 1e-06)
    return (widened * inverse_rms * norm_gain[:, None]).astype(jnp.bfloat16)


def swap_blocks(shard, z_count, core_count):
    pairs = [
        ((z * core_count + core) * z_count + p, (p * core_count + core) * z_count + z)
        for z in range(z_count)
        for core in range(core_count)
        for p in range(z_count)
    ]
    return lax.ppermute(shard, ZC + XY, pairs)


def on_device(inputs, targets, norm_gain, gate_weight, up_weight, down_weight, neighbours):
    token_count = inputs.shape[1]
    param_count = lax.axis_size(XY)
    z_count = lax.axis_size("z")
    core_count = lax.axis_size("core")
    client_count = z_count * core_count
    factor = 1.0 / math.sqrt(token_count)
    features = param_count * inputs.shape[2]
    slice_rows = features // client_count
    hidden_units = gate_weight.shape[1]

    own_inputs = inputs[0].T
    met_inputs = lax.all_gather(own_inputs, "z", axis=0, tiled=False)
    gathered = gather_rows(own_inputs, XY, param_count)
    normed = rms_normed(gathered, norm_gain)
    gate_value = contract(gate_weight, normed, 0, 0)
    up_value = contract(up_weight, normed, 0, 0)
    hidden = (gelu_tanh(gate_value) * up_value).astype(jnp.bfloat16)
    partial_out = contract(down_weight, hidden, 0, 0).astype(jnp.bfloat16)
    parts = exchange(
        partial_out.reshape(param_count, features // param_count, token_count), XY
    )
    summed = jnp.sum(parts.astype(jnp.float32), axis=0)
    own_residual = ((summed - targets[0].T.astype(jnp.float32)) * factor).astype(jnp.bfloat16)
    met_residual = swap_blocks(own_residual, z_count, core_count)
    met_residual = lax.all_gather(met_residual, "z", axis=0, tiled=True)

    share = hidden_units // z_count
    height = -(-3 * share // 8) * 8
    first = lax.axis_index("z") * share
    column = lax.axis_index("core") * (features // core_count)

    def own_part(rows):
        return lax.dynamic_slice(rows, (first, column), (share, features // core_count))

    part = jnp.concatenate(
        [
            own_part(gate_weight.T),
            own_part(up_weight.T),
            own_part(down_weight),
            jnp.zeros((height - 3 * share, features // core_count), jnp.bfloat16),
        ],
        axis=0,
    )
    part, own_residual = lax.optimization_barrier((part, own_residual))
    part = gather_rows(part, XY, param_count)
    part, met_inputs = lax.optimization_barrier((part, met_inputs))
    weights_met = gather_rows(part[None], "core", core_count)
    met_inputs = exchange(met_inputs, XY).reshape(features, token_count)
    met_normed = rms_normed(met_inputs, norm_gain)

    def times_weights(rows):
        halves = rows.reshape(core_count, features // core_count, token_count)
        total = sum(contract(weights_met[core], halves[core], 1, 0) for core in range(core_count))
        return total.reshape(param_count, height, token_count)

    values = times_weights(met_normed)
    values, met_residual = lax.optimization_barrier((values, met_residual))
    activated, gelu_back = jax.vjp(gelu_tanh, values[:, :share])
    up_value = values[:, share : 2 * share]
    hidden = (activated * up_value).astype(jnp.bfloat16)
    back_hidden = times_weights(met_residual)[:, 2 * share : 3 * share]
    back_gate = gelu_back(back_hidden * up_value)[0].astype(jnp.bfloat16)
    back_up = (back_hidden * activated).astype(jnp.bfloat16)
    rest = jnp.zeros((param_count, height - 3 * share, token_count), jnp.bfloat16)
    none = jnp.zeros((param_count, share, token_count), jnp.bfloat16)
    left = jnp.concatenate(
        [
            jnp.concatenate([back_gate, back_up, none, rest], axis=1),
            jnp.concatenate([none, none, hidden, rest], axis=1),
        ],
        axis=2,
    ).reshape(param_count * height, 2 * token_count)
    right = jnp.concatenate([met_normed, met_residual], axis=1)
    right = right.reshape(z_count, core_count, slice_rows, 2 * token_count)
    half = z_count * slice_rows
    deltas = [
        (-contract(left, right[:, core].reshape(half, 2 * token_count), 1, 1))
        .astype(jnp.bfloat16)
        .reshape(param_count, height, half)
        for core in range(core_count)
    ]
    owned = exchange(jnp.concatenate(deltas, axis=0), ("core",) + XY)

    gram = pair_products(owned).reshape(8, -1)
    gram = sum_over(gram, ("core",) + XY, core_count * param_count)
    gram = sum_over(gram, "z", z_count).reshape(client_count, client_count)
    weights = krum_weights(gram, neighbours.reshape(z_count, core_count).T.reshape(-1))
    update = jnp.sum(weights[:, None, None] * owned.astype(jnp.float32), axis=0)
    update = update.astype(jnp.bfloat16).reshape(height, z_count, slice_rows).swapaxes(0, 1)
    update = exchange(update, "z").astype(jnp.float32)

    def placed(index):
        rows = update[:, index * share : (index + 1) * share]
        return rows.reshape(hidden_units, slice_rows).T

    return (
        placed(0),
        placed(1),
        placed(2),
        client_count * weights.reshape(core_count, z_count).T.reshape(-1),
    )


def solution(mesh):
    torus = Mesh(mesh.devices.reshape(16, 2, 4, 4), ("z", "core", "x", "y"))
    in_specs = (
        P(ZC, None, XY),
        P(ZC, None, XY),
        P(),
        P(None, XY),
        P(None, XY),
        P(XY, None),
        P(),
    )
    out_specs = (P(ZC, XY), P(ZC, XY), P(ZC, XY), P())
    return jax.shard_map(
        on_device, mesh=torus, in_specs=in_specs, out_specs=out_specs, check_vma=False
    )
```

```python
import math

import jax
import jax.numpy as jnp
from jax import lax
from jax.experimental import pallas as pl
from jax.experimental.pallas import tpu as pltpu
from jax.sharding import Mesh, PartitionSpec as P


XY = ("x", "y")
ZC = ("z", "core")


def gelu_tanh(values):
    return jax.nn.gelu(values, approximate=True)


def exchange(blocks, axes):
    return lax.all_to_all(blocks, axes, split_axis=0, concat_axis=0, tiled=True)


def gather_rows(shard, axes, count):
    copies = jnp.broadcast_to(shard[None], (count,) + shard.shape)
    return exchange(copies, axes).reshape((count * shard.shape[0],) + shard.shape[1:])


def contract(left, right, left_dim, right_dim):
    return lax.dot_general(
        left, right, (((left_dim,), (right_dim,)), ((), ())), preferred_element_type=jnp.float32
    )


def exact_dot(left, right, left_dim, right_dim):
    return lax.dot_general(
        left, right, (((left_dim,), (right_dim,)), ((), ())),
        precision=lax.Precision.HIGHEST, preferred_element_type=jnp.float32,
    )


def lane_place(index, size, lanes):
    row = lax.broadcasted_iota(jnp.int32, (size, lanes), 0)
    column = lax.broadcasted_iota(jnp.int32, (size, lanes), 1)
    return (column == row + index * size).astype(jnp.float32)


def gram_kernel(block_ref, copies_ref, total_ref):
    clients, rows, columns = block_ref.shape
    tall = 8
    size = clients * tall
    total_ref[...] = jnp.zeros_like(total_ref)

    @pl.loop(0, rows // tall)
    def _(index):
        start = pl.multiple_of(index * tall, tall)
        tile = block_ref[:, pl.ds(start, tall), :].reshape(size, columns)
        total_ref[...] += contract(tile, tile, 1, 1)

    row_index = lax.broadcasted_iota(jnp.int32, (size, size), 0)
    col_index = lax.broadcasted_iota(jnp.int32, (size, size), 1)
    kept = jnp.where(row_index % tall == col_index % tall, total_ref[...], 0.0)
    pick_client = lax.broadcasted_iota(jnp.int32, (clients, size), 0)
    pick_row = lax.broadcasted_iota(jnp.int32, (clients, size), 1) // tall
    pick = (pick_row == pick_client).astype(jnp.float32)
    gram = exact_dot(exact_dot(pick, kept, 1, 0), pick, 1, 1)
    packed = jnp.zeros(copies_ref.shape[1:], jnp.float32)
    for index in range(clients // tall):
        packed += exact_dot(
            gram[index * tall : (index + 1) * tall],
            lane_place(index, clients, copies_ref.shape[2]), 1, 0,
        )
    copies_ref[...] = jnp.broadcast_to(packed[None], copies_ref.shape)


def pair_products(exchanged, copies):
    clients, rows, columns = exchanged.shape
    return pl.pallas_call(
        gram_kernel,
        out_shape=jax.ShapeDtypeStruct((copies, 8, 128), jnp.float32),
        in_specs=[pl.BlockSpec(memory_space=pltpu.VMEM)],
        out_specs=pl.BlockSpec(memory_space=pltpu.VMEM),
        scratch_shapes=[pltpu.VMEM((clients * 8, clients * 8), jnp.float32)],
        cost_estimate=pl.CostEstimate(
            flops=2 * rows * clients * clients * 8 * columns,
            bytes_accessed=2 * clients * rows * columns,
            transcendentals=0,
        ),
        name="pair_products",
    )(exchanged)


def finish_kernel(parts_ref, neighbours_ref, owned_ref, update_ref, relative_ref):
    clients, rows, columns = owned_ref.shape
    pieces, _, width = update_ref.shape
    tall = 8
    packed = jnp.sum(parts_ref[...], axis=0)
    gram = jnp.concatenate(
        [
            exact_dot(packed, lane_place(index, clients, packed.shape[1]), 1, 1)
            for index in range(clients // tall)
        ],
        axis=0,
    )
    row_index = lax.broadcasted_iota(jnp.int32, (clients, clients), 0)
    col_index = lax.broadcasted_iota(jnp.int32, (clients, clients), 1)
    same = row_index == col_index
    diagonal = jnp.where(same, gram, 0.0)
    distance = (
        jnp.sum(diagonal, axis=1, keepdims=True)
        + jnp.sum(diagonal, axis=0, keepdims=True)
        - 2.0 * gram
    )
    distance = jnp.where(same, 1e30, distance)
    rank = jnp.zeros((clients, clients), jnp.float32)
    for index in range(clients):
        rival = distance[:, index : index + 1]
        ahead = (rival < distance) | ((rival == distance) & (index < col_index))
        rank += jnp.where(ahead, 1.0, 0.0)
    count = jnp.sum(
        jnp.where(same, neighbours_ref[...].astype(jnp.float32), 0.0), axis=1, keepdims=True
    )
    scores = jnp.sum(jnp.where(rank < count, distance, 0.0), axis=1, keepdims=True)
    mean = jnp.sum(scores, axis=0, keepdims=True) / clients
    exponent = jnp.exp(-4.0 * (scores / mean))
    weights = exponent / jnp.sum(exponent, axis=0, keepdims=True)
    relative_ref[...] = clients * jnp.sum(jnp.where(same, weights, 0.0), axis=0, keepdims=True)
    for start in range(0, rows, tall):
        total = jnp.zeros((tall, columns), jnp.float32)
        for index in range(clients):
            total += weights[index : index + 1, :] * owned_ref[
                index, start : start + tall, :
            ].astype(jnp.float32)
        total = total.astype(update_ref.dtype)
        for piece in range(pieces):
            update_ref[piece, start : start + tall, :] = total[
                :, piece * width : (piece + 1) * width
            ]


def finish(parts, neighbours, owned, pieces):
    clients, rows, columns = owned.shape
    vmem = pl.BlockSpec(memory_space=pltpu.VMEM)
    return pl.pallas_call(
        finish_kernel,
        in_specs=[vmem] * 3,
        out_specs=[vmem] * 2,
        out_shape=[
            jax.ShapeDtypeStruct((pieces, rows, columns // pieces), jnp.bfloat16),
            jax.ShapeDtypeStruct((1, clients), jnp.float32),
        ],
        cost_estimate=pl.CostEstimate(
            flops=2 * clients * rows * columns,
            bytes_accessed=2 * clients * rows * columns + 2 * rows * columns,
            transcendentals=clients,
        ),
        name="finish",
    )(parts, neighbours, owned)


def delta_kernel(left_ref, other_left_ref, right_ref, other_right_ref, out_ref):
    planes, _, rows, tokens = right_ref.shape
    right = right_ref[...].reshape(planes * rows, tokens)
    other_right = other_right_ref[...].reshape(planes * rows, tokens)
    total = contract(left_ref[...], right, 1, 1) + contract(other_left_ref[...], other_right, 1, 1)
    out_ref[...] = (-total).astype(out_ref.dtype).reshape(out_ref.shape)


def make_deltas(left, other_left, right, other_right, height):
    planes, cores, rows, tokens = right.shape
    slices = left.shape[0] // height
    chunks = 2
    tall = left.shape[0] // chunks
    left_spec = pl.BlockSpec((tall, tokens), lambda core, chunk: (chunk, 0))
    right_spec = pl.BlockSpec((planes, 1, rows, tokens), lambda core, chunk: (0, core, 0, 0))
    return pl.pallas_call(
        delta_kernel,
        grid=(cores, chunks),
        in_specs=[left_spec, left_spec, right_spec, right_spec],
        out_specs=pl.BlockSpec(
            (slices // chunks, height, planes * rows), lambda core, chunk: (core * chunks + chunk, 0, 0)
        ),
        out_shape=jax.ShapeDtypeStruct((cores * slices, height, planes * rows), jnp.bfloat16),
        cost_estimate=pl.CostEstimate(
            flops=4 * left.shape[0] * planes * cores * rows * tokens,
            bytes_accessed=4 * (left.shape[0] + planes * cores * rows) * tokens
            + 2 * left.shape[0] * planes * cores * rows,
            transcendentals=0,
        ),
        name="make_deltas",
    )(left, other_left, right, other_right)


def rms_normed(raw, norm_gain):
    widened = raw.astype(jnp.float32)
    inverse_rms = lax.rsqrt(jnp.mean(widened * widened, axis=0, keepdims=True) + 1e-06)
    return (widened * inverse_rms * norm_gain[:, None]).astype(jnp.bfloat16)


def swap_blocks(shard, z_count, core_count):
    pairs = [
        ((z * core_count + core) * z_count + p, (p * core_count + core) * z_count + z)
        for z in range(z_count)
        for core in range(core_count)
        for p in range(z_count)
    ]
    return lax.ppermute(shard, ZC + XY, pairs)


def on_device(inputs, targets, norm_gain, gate_weight, up_weight, down_weight, neighbours):
    token_count = inputs.shape[1]
    param_count = lax.axis_size(XY)
    z_count = lax.axis_size("z")
    core_count = lax.axis_size("core")
    client_count = z_count * core_count
    factor = 1.0 / math.sqrt(token_count)
    features = param_count * inputs.shape[2]
    slice_rows = features // client_count
    hidden_units = gate_weight.shape[1]

    own_inputs = inputs[0].T
    met_inputs = lax.all_gather(own_inputs, "z", axis=0, tiled=False)
    gathered = gather_rows(own_inputs, XY, param_count)
    normed = rms_normed(gathered, norm_gain)
    gate_value = contract(gate_weight, normed, 0, 0)
    up_value = contract(up_weight, normed, 0, 0)
    hidden = (gelu_tanh(gate_value) * up_value).astype(jnp.bfloat16)
    partial_out = contract(down_weight, hidden, 0, 0).astype(jnp.bfloat16)
    parts = exchange(
        partial_out.reshape(param_count, features // param_count, token_count), XY
    )
    summed = jnp.sum(parts.astype(jnp.float32), axis=0)
    own_residual = ((summed - targets[0].T.astype(jnp.float32)) * factor).astype(jnp.bfloat16)
    met_residual = swap_blocks(own_residual, z_count, core_count)
    met_residual = lax.all_gather(met_residual, "z", axis=0, tiled=True)

    share = hidden_units // z_count
    height = -(-3 * share // 8) * 8
    first = lax.axis_index("z") * share
    column = lax.axis_index("core") * (features // core_count)

    def own_part(rows):
        return lax.dynamic_slice(rows, (first, column), (share, features // core_count))

    group = -(-share // 8) * 8
    fill = jnp.zeros((group - share, features // core_count), jnp.bfloat16)
    part = jnp.concatenate(
        [own_part(gate_weight.T), fill, own_part(up_weight.T), fill, own_part(down_weight), fill],
        axis=0,
    )
    part, own_residual = lax.optimization_barrier((part, own_residual))
    part = gather_rows(part, XY, param_count)
    part, met_inputs = lax.optimization_barrier((part, met_inputs))
    other = lax.ppermute(part, "core", [(0, 1), (1, 0)])
    met_inputs = exchange(met_inputs, XY).reshape(features, token_count)
    low = lax.axis_index("core") == 0
    met_weights = jnp.concatenate(
        [jnp.where(low, part, other), jnp.where(low, other, part)], axis=1
    ).reshape(param_count, 3 * group, features)
    ahead_weights = met_weights[:, : 2 * group].reshape(2 * param_count * group, features)
    back_weights = met_weights[:, 2 * group :].reshape(param_count * group, features)
    met_normed = rms_normed(met_inputs, norm_gain)
    values = contract(ahead_weights, met_normed, 1, 0)
    values, back_weights, met_residual = lax.optimization_barrier(
        (values, back_weights, met_residual)
    )
    values = values.reshape(param_count, 2 * group, token_count)
    activated, gelu_back = jax.vjp(gelu_tanh, values[:, :share])
    up_value = values[:, group : group + share]
    hidden = (activated * up_value).astype(jnp.bfloat16)
    back_hidden = contract(back_weights, met_residual, 1, 0)
    back_hidden = back_hidden.reshape(param_count, group, token_count)[:, :share]
    back_gate = gelu_back(back_hidden * up_value)[0].astype(jnp.bfloat16)
    back_up = (back_hidden * activated).astype(jnp.bfloat16)
    rest = jnp.zeros((param_count, height - 3 * share, token_count), jnp.bfloat16)
    none = jnp.zeros((param_count, share, token_count), jnp.bfloat16)
    flat = (param_count * height, token_count)
    by_plane = (z_count, core_count, slice_rows, token_count)
    deltas = make_deltas(
        jnp.concatenate([back_gate, back_up, none, rest], axis=1).reshape(flat),
        jnp.concatenate([none, none, hidden, rest], axis=1).reshape(flat),
        met_normed.reshape(by_plane),
        met_residual.reshape(by_plane),
        height,
    )
    owned = exchange(deltas, ("core",) + XY)

    gram = pair_products(owned, core_count * param_count)
    gram = jnp.sum(exchange(gram, ("core",) + XY), axis=0)
    gram = exchange(jnp.broadcast_to(gram[None], (z_count,) + gram.shape), "z")
    order = neighbours.reshape(z_count, core_count).T.reshape(1, -1)
    update, relative = finish(gram, order, owned, z_count)
    update = exchange(update, "z").astype(jnp.float32)

    def placed(index):
        rows = update[:, index * share : (index + 1) * share]
        return rows.reshape(hidden_units, slice_rows).T

    return (
        placed(0),
        placed(1),
        placed(2),
        relative.reshape(core_count, z_count).T.reshape(-1),
    )


def solution(mesh):
    torus = Mesh(mesh.devices.reshape(16, 2, 4, 4), ("z", "core", "x", "y"))
    in_specs = (
        P(ZC, None, XY),
        P(ZC, None, XY),
        P(),
        P(None, XY),
        P(None, XY),
        P(XY, None),
        P(),
    )
    out_specs = (P(ZC, XY), P(ZC, XY), P(ZC, XY), P())
    return jax.shard_map(
        on_device, mesh=torus, in_specs=in_specs, out_specs=out_specs, check_vma=False
    )
```

```python
import math

import jax
import jax.numpy as jnp
from jax import lax
from jax.experimental import pallas as pl
from jax.experimental.pallas import tpu as pltpu
from jax.sharding import Mesh, PartitionSpec as P


XY = ("x", "y")
ZC = ("z", "core")


def gelu_tanh(values):
    return jax.nn.gelu(values, approximate=True)


def exchange(blocks, axes):
    return lax.all_to_all(blocks, axes, split_axis=0, concat_axis=0, tiled=True)


def gather_rows(shard, axes, count):
    copies = jnp.broadcast_to(shard[None], (count,) + shard.shape)
    return exchange(copies, axes).reshape((count * shard.shape[0],) + shard.shape[1:])


def contract(left, right, left_dim, right_dim):
    return lax.dot_general(
        left, right, (((left_dim,), (right_dim,)), ((), ())), preferred_element_type=jnp.float32
    )


def exact_dot(left, right, left_dim, right_dim):
    return lax.dot_general(
        left, right, (((left_dim,), (right_dim,)), ((), ())),
        precision=lax.Precision.HIGHEST, preferred_element_type=jnp.float32,
    )


def lane_place(index, size, lanes):
    row = lax.broadcasted_iota(jnp.int32, (size, lanes), 0)
    column = lax.broadcasted_iota(jnp.int32, (size, lanes), 1)
    return (column == row + index * size).astype(jnp.float32)


def gram_kernel(block_ref, copies_ref, total_ref):
    clients, rows, columns = block_ref.shape
    tall = 8
    size = clients * tall
    total_ref[...] = jnp.zeros_like(total_ref)

    @pl.loop(0, rows // tall)
    def _(index):
        start = pl.multiple_of(index * tall, tall)
        tile = block_ref[:, pl.ds(start, tall), :].reshape(size, columns)
        total_ref[...] += contract(tile, tile, 1, 1)

    row_index = lax.broadcasted_iota(jnp.int32, (size, size), 0)
    col_index = lax.broadcasted_iota(jnp.int32, (size, size), 1)
    kept = jnp.where(row_index % tall == col_index % tall, total_ref[...], 0.0)
    pick_client = lax.broadcasted_iota(jnp.int32, (clients, size), 0)
    pick_row = lax.broadcasted_iota(jnp.int32, (clients, size), 1) // tall
    pick = (pick_row == pick_client).astype(jnp.float32)
    gram = exact_dot(exact_dot(pick, kept, 1, 0), pick, 1, 1)
    packed = jnp.zeros(copies_ref.shape[1:], jnp.float32)
    for index in range(clients // tall):
        packed += exact_dot(
            gram[index * tall : (index + 1) * tall],
            lane_place(index, clients, copies_ref.shape[2]), 1, 0,
        )
    copies_ref[...] = jnp.broadcast_to(packed[None], copies_ref.shape)


def pair_products(exchanged, copies):
    clients, rows, columns = exchanged.shape
    return pl.pallas_call(
        gram_kernel,
        out_shape=jax.ShapeDtypeStruct((copies, 8, 128), jnp.float32),
        in_specs=[pl.BlockSpec(memory_space=pltpu.VMEM)],
        out_specs=pl.BlockSpec(memory_space=pltpu.VMEM),
        scratch_shapes=[pltpu.VMEM((clients * 8, clients * 8), jnp.float32)],
        cost_estimate=pl.CostEstimate(
            flops=2 * rows * clients * clients * 8 * columns,
            bytes_accessed=2 * clients * rows * columns,
            transcendentals=0,
        ),
        name="pair_products",
    )(exchanged)


def finish_kernel(parts_ref, neighbours_ref, owned_ref, update_ref, relative_ref):
    clients, rows, columns = owned_ref.shape
    pieces, _, width = update_ref.shape
    tall = 8
    packed = jnp.sum(parts_ref[...], axis=0)
    gram = jnp.concatenate(
        [
            exact_dot(packed, lane_place(index, clients, packed.shape[1]), 1, 1)
            for index in range(clients // tall)
        ],
        axis=0,
    )
    row_index = lax.broadcasted_iota(jnp.int32, (clients, clients), 0)
    col_index = lax.broadcasted_iota(jnp.int32, (clients, clients), 1)
    same = row_index == col_index
    diagonal = jnp.where(same, gram, 0.0)
    distance = (
        jnp.sum(diagonal, axis=1, keepdims=True)
        + jnp.sum(diagonal, axis=0, keepdims=True)
        - 2.0 * gram
    )
    distance = jnp.where(same, 1e30, distance)
    rank = jnp.zeros((clients, clients), jnp.float32)
    for index in range(clients):
        rival = distance[:, index : index + 1]
        ahead = (rival < distance) | ((rival == distance) & (index < col_index))
        rank += jnp.where(ahead, 1.0, 0.0)
    count = jnp.sum(
        jnp.where(same, neighbours_ref[...].astype(jnp.float32), 0.0), axis=1, keepdims=True
    )
    scores = jnp.sum(jnp.where(rank < count, distance, 0.0), axis=1, keepdims=True)
    mean = jnp.sum(scores, axis=0, keepdims=True) / clients
    exponent = jnp.exp(-4.0 * (scores / mean))
    weights = exponent / jnp.sum(exponent, axis=0, keepdims=True)
    relative_ref[...] = clients * jnp.sum(jnp.where(same, weights, 0.0), axis=0, keepdims=True)
    for start in range(0, rows, tall):
        total = jnp.zeros((tall, columns), jnp.float32)
        for index in range(clients):
            total += weights[index : index + 1, :] * owned_ref[
                index, start : start + tall, :
            ].astype(jnp.float32)
        total = total.astype(update_ref.dtype)
        for piece in range(pieces):
            update_ref[piece, start : start + tall, :] = total[
                :, piece * width : (piece + 1) * width
            ]


def finish(parts, neighbours, owned, pieces):
    clients, rows, columns = owned.shape
    vmem = pl.BlockSpec(memory_space=pltpu.VMEM)
    return pl.pallas_call(
        finish_kernel,
        in_specs=[vmem] * 3,
        out_specs=[vmem] * 2,
        out_shape=[
            jax.ShapeDtypeStruct((pieces, rows, columns // pieces), jnp.bfloat16),
            jax.ShapeDtypeStruct((1, clients), jnp.float32),
        ],
        cost_estimate=pl.CostEstimate(
            flops=2 * clients * rows * columns,
            bytes_accessed=2 * clients * rows * columns + 2 * rows * columns,
            transcendentals=clients,
        ),
        name="finish",
    )(parts, neighbours, owned)


def delta_kernel(ahead_ref, back_ref, normed_ref, residual_ref, out_ref):
    planes, _, rows, tokens = normed_ref.shape
    slices, ahead_rows, _ = ahead_ref.shape
    back_rows = back_ref.shape[1]
    columns = planes * rows
    shared = ahead_rows + back_rows - out_ref.shape[1]
    ahead = contract(
        ahead_ref[...].reshape(slices * ahead_rows, tokens),
        normed_ref[...].reshape(columns, tokens), 1, 1,
    ).reshape(slices, ahead_rows, columns)
    back = contract(
        back_ref[...].reshape(slices * back_rows, tokens),
        residual_ref[...].reshape(columns, tokens), 1, 1,
    ).reshape(slices, back_rows, columns)
    first = ahead_rows - shared
    out_ref[:, :first, :] = (-ahead[:, :first]).astype(out_ref.dtype)
    both = ahead[:, first:] + back[:, :shared]
    out_ref[:, first:ahead_rows, :] = (-both).astype(out_ref.dtype)
    out_ref[:, ahead_rows:, :] = (-back[:, shared:]).astype(out_ref.dtype)


def make_deltas(ahead, back, normed, residual, height):
    planes, cores, rows, tokens = normed.shape
    slices = ahead.shape[0]
    whole = lambda left: pl.BlockSpec(left.shape, lambda core: (0, 0, 0))
    right_spec = pl.BlockSpec((planes, 1, rows, tokens), lambda core: (0, core, 0, 0))
    return pl.pallas_call(
        delta_kernel,
        grid=(cores,),
        in_specs=[whole(ahead), whole(back), right_spec, right_spec],
        out_specs=pl.BlockSpec((slices, height, planes * rows), lambda core: (core, 0, 0)),
        out_shape=jax.ShapeDtypeStruct((cores * slices, height, planes * rows), jnp.bfloat16),
        cost_estimate=pl.CostEstimate(
            flops=2 * slices * (ahead.shape[1] + back.shape[1]) * planes * cores * rows * tokens,
            bytes_accessed=4 * planes * cores * rows * tokens
            + 2 * slices * height * planes * cores * rows,
            transcendentals=0,
        ),
        name="make_deltas",
    )(ahead, back, normed, residual)


def rms_normed(raw, norm_gain):
    widened = raw.astype(jnp.float32)
    inverse_rms = lax.rsqrt(jnp.mean(widened * widened, axis=0, keepdims=True) + 1e-06)
    return (widened * inverse_rms * norm_gain[:, None]).astype(jnp.bfloat16)


def swap_blocks(shard, z_count, core_count):
    pairs = [
        ((z * core_count + core) * z_count + p, (p * core_count + core) * z_count + z)
        for z in range(z_count)
        for core in range(core_count)
        for p in range(z_count)
    ]
    return lax.ppermute(shard, ZC + XY, pairs)


def on_device(inputs, targets, norm_gain, gate_weight, up_weight, down_weight, neighbours):
    token_count = inputs.shape[1]
    param_count = lax.axis_size(XY)
    z_count = lax.axis_size("z")
    core_count = lax.axis_size("core")
    client_count = z_count * core_count
    factor = 1.0 / math.sqrt(token_count)
    features = param_count * inputs.shape[2]
    slice_rows = features // client_count
    hidden_units = gate_weight.shape[1]

    own_inputs = inputs[0].T
    met_inputs = lax.all_gather(own_inputs, "z", axis=0, tiled=False)
    gathered = gather_rows(own_inputs, XY, param_count)
    normed = rms_normed(gathered, norm_gain)
    gate_value = contract(gate_weight, normed, 0, 0)
    up_value = contract(up_weight, normed, 0, 0)
    hidden = (gelu_tanh(gate_value) * up_value).astype(jnp.bfloat16)
    partial_out = contract(down_weight, hidden, 0, 0).astype(jnp.bfloat16)
    parts = exchange(
        partial_out.reshape(param_count, features // param_count, token_count), XY
    )
    summed = jnp.sum(parts.astype(jnp.float32), axis=0)
    own_residual = ((summed - targets[0].T.astype(jnp.float32)) * factor).astype(jnp.bfloat16)
    met_residual = swap_blocks(own_residual, z_count, core_count)
    met_residual = lax.all_gather(met_residual, "z", axis=0, tiled=True)

    share = hidden_units // z_count
    height = -(-3 * share // 8) * 8
    first = lax.axis_index("z") * share
    column = lax.axis_index("core") * (features // core_count)

    def own_part(rows):
        return lax.dynamic_slice(rows, (first, column), (share, features // core_count))

    ahead_rows = -(-2 * share // 8) * 8
    back_rows = -(-share // 8) * 8

    def fill(rows):
        return jnp.zeros((rows, features // core_count), jnp.bfloat16)

    part = jnp.concatenate(
        [
            own_part(gate_weight.T),
            own_part(up_weight.T),
            fill(ahead_rows - 2 * share),
            own_part(down_weight),
            fill(back_rows - share),
        ],
        axis=0,
    )
    part, own_residual = lax.optimization_barrier((part, own_residual))
    part = gather_rows(part, XY, param_count)
    part, met_inputs = lax.optimization_barrier((part, met_inputs))
    other = lax.ppermute(part, "core", [(0, 1), (1, 0)])
    met_inputs = exchange(met_inputs, XY).reshape(features, token_count)
    low = lax.axis_index("core") == 0
    met_weights = jnp.concatenate(
        [jnp.where(low, part, other), jnp.where(low, other, part)], axis=1
    ).reshape(param_count, ahead_rows + back_rows, features)
    ahead_weights = met_weights[:, :ahead_rows].reshape(param_count * ahead_rows, features)
    back_weights = met_weights[:, ahead_rows:].reshape(param_count * back_rows, features)
    met_normed = rms_normed(met_inputs, norm_gain)
    values = contract(ahead_weights, met_normed, 1, 0)
    values, back_weights, met_residual = lax.optimization_barrier(
        (values, back_weights, met_residual)
    )
    values = values.reshape(param_count, ahead_rows, token_count)
    activated, gelu_back = jax.vjp(gelu_tanh, values[:, :share])
    up_value = values[:, share : 2 * share]
    hidden = (activated * up_value).astype(jnp.bfloat16)
    back_hidden = contract(back_weights, met_residual, 1, 0)
    back_hidden = back_hidden.reshape(param_count, back_rows, token_count)[:, :share]
    back_gate = gelu_back(back_hidden * up_value)[0].astype(jnp.bfloat16)
    back_up = (back_hidden * activated).astype(jnp.bfloat16)

    def blank(rows):
        return jnp.zeros((param_count, rows, token_count), jnp.bfloat16)

    lead = 2 * share - (height - back_rows)
    by_plane = (z_count, core_count, slice_rows, token_count)
    deltas = make_deltas(
        jnp.concatenate([back_gate, back_up, blank(ahead_rows - 2 * share)], axis=1),
        jnp.concatenate([blank(lead), hidden, blank(back_rows - share - lead)], axis=1),
        met_normed.reshape(by_plane),
        met_residual.reshape(by_plane),
        height,
    )
    owned = exchange(deltas, ("core",) + XY)

    gram = pair_products(owned, core_count * param_count)
    gram = jnp.sum(exchange(gram, ("core",) + XY), axis=0)
    gram = exchange(jnp.broadcast_to(gram[None], (z_count,) + gram.shape), "z")
    order = neighbours.reshape(z_count, core_count).T.reshape(1, -1)
    update, relative = finish(gram, order, owned, z_count)
    update = exchange(update, "z").astype(jnp.float32)

    def placed(index):
        rows = update[:, index * share : (index + 1) * share]
        return rows.reshape(hidden_units, slice_rows).T

    return (
        placed(0),
        placed(1),
        placed(2),
        relative.reshape(core_count, z_count).T.reshape(-1),
    )


def solution(mesh):
    torus = Mesh(mesh.devices.reshape(16, 2, 4, 4), ("z", "core", "x", "y"))
    in_specs = (
        P(ZC, None, XY),
        P(ZC, None, XY),
        P(),
        P(None, XY),
        P(None, XY),
        P(XY, None),
        P(),
    )
    out_specs = (P(ZC, XY), P(ZC, XY), P(ZC, XY), P())
    return jax.shard_map(
        on_device, mesh=torus, in_specs=in_specs, out_specs=out_specs, check_vma=False
    )
```

```python
import math

import jax
import jax.numpy as jnp
from jax import lax
from jax.experimental import pallas as pl
from jax.experimental.pallas import tpu as pltpu
from jax.sharding import Mesh, PartitionSpec as P


XY = ("x", "y")
ZC = ("z", "core")


def gelu_tanh(values):
    return jax.nn.gelu(values, approximate=True)


def exchange(blocks, axes):
    return lax.all_to_all(blocks, axes, split_axis=0, concat_axis=0, tiled=True)


def gather_rows(shard, axes, count):
    copies = jnp.broadcast_to(shard[None], (count,) + shard.shape)
    return exchange(copies, axes).reshape((count * shard.shape[0],) + shard.shape[1:])


def contract(left, right, left_dim, right_dim):
    return lax.dot_general(
        left, right, (((left_dim,), (right_dim,)), ((), ())), preferred_element_type=jnp.float32
    )


def exact_dot(left, right, left_dim, right_dim):
    return lax.dot_general(
        left, right, (((left_dim,), (right_dim,)), ((), ())),
        precision=lax.Precision.HIGHEST, preferred_element_type=jnp.float32,
    )


def lane_place(index, size, lanes):
    row = lax.broadcasted_iota(jnp.int32, (size, lanes), 0)
    column = lax.broadcasted_iota(jnp.int32, (size, lanes), 1)
    return (column == row + index * size).astype(jnp.float32)


def gram_kernel(block_ref, copies_ref, total_ref):
    clients, rows, columns = block_ref.shape
    tall = 8
    size = clients * tall
    total_ref[...] = jnp.zeros_like(total_ref)

    @pl.loop(0, rows // tall)
    def _(index):
        start = pl.multiple_of(index * tall, tall)
        tile = block_ref[:, pl.ds(start, tall), :].reshape(size, columns)
        total_ref[...] += contract(tile, tile, 1, 1)

    row_index = lax.broadcasted_iota(jnp.int32, (size, size), 0)
    col_index = lax.broadcasted_iota(jnp.int32, (size, size), 1)
    kept = jnp.where(row_index % tall == col_index % tall, total_ref[...], 0.0)
    pick_client = lax.broadcasted_iota(jnp.int32, (clients, size), 0)
    pick_row = lax.broadcasted_iota(jnp.int32, (clients, size), 1) // tall
    pick = (pick_row == pick_client).astype(jnp.float32)
    gram = exact_dot(exact_dot(pick, kept, 1, 0), pick, 1, 1)
    packed = jnp.zeros(copies_ref.shape[1:], jnp.float32)
    for index in range(clients // tall):
        packed += exact_dot(
            gram[index * tall : (index + 1) * tall],
            lane_place(index, clients, copies_ref.shape[2]), 1, 0,
        )
    copies_ref[...] = jnp.broadcast_to(packed[None], copies_ref.shape)


def pair_products(exchanged, copies):
    clients, rows, columns = exchanged.shape
    return pl.pallas_call(
        gram_kernel,
        out_shape=jax.ShapeDtypeStruct((copies, 8, 128), jnp.float32),
        in_specs=[pl.BlockSpec(memory_space=pltpu.VMEM)],
        out_specs=pl.BlockSpec(memory_space=pltpu.VMEM),
        scratch_shapes=[pltpu.VMEM((clients * 8, clients * 8), jnp.float32)],
        cost_estimate=pl.CostEstimate(
            flops=2 * rows * clients * clients * 8 * columns,
            bytes_accessed=2 * clients * rows * columns,
            transcendentals=0,
        ),
        name="pair_products",
    )(exchanged)


def finish_kernel(parts_ref, neighbours_ref, owned_ref, update_ref, relative_ref):
    clients, rows, columns = owned_ref.shape
    pieces, _, width = update_ref.shape
    tall = 8
    packed = jnp.sum(parts_ref[...], axis=0)
    gram = jnp.concatenate(
        [
            exact_dot(packed, lane_place(index, clients, packed.shape[1]), 1, 1)
            for index in range(clients // tall)
        ],
        axis=0,
    )
    row_index = lax.broadcasted_iota(jnp.int32, (clients, clients), 0)
    col_index = lax.broadcasted_iota(jnp.int32, (clients, clients), 1)
    same = row_index == col_index
    diagonal = jnp.where(same, gram, 0.0)
    distance = (
        jnp.sum(diagonal, axis=1, keepdims=True)
        + jnp.sum(diagonal, axis=0, keepdims=True)
        - 2.0 * gram
    )
    distance = jnp.where(same, 1e30, distance)
    rank = jnp.zeros((clients, clients), jnp.float32)
    for index in range(clients):
        rival = distance[:, index : index + 1]
        ahead = (rival < distance) | ((rival == distance) & (index < col_index))
        rank += jnp.where(ahead, 1.0, 0.0)
    count = jnp.sum(
        jnp.where(same, neighbours_ref[...].astype(jnp.float32), 0.0), axis=1, keepdims=True
    )
    scores = jnp.sum(jnp.where(rank < count, distance, 0.0), axis=1, keepdims=True)
    mean = jnp.sum(scores, axis=0, keepdims=True) / clients
    exponent = jnp.exp(-4.0 * (scores / mean))
    weights = exponent / jnp.sum(exponent, axis=0, keepdims=True)
    relative_ref[...] = clients * jnp.sum(jnp.where(same, weights, 0.0), axis=0, keepdims=True)
    for start in range(0, rows, tall):
        total = jnp.zeros((tall, columns), jnp.float32)
        for index in range(clients):
            total += weights[index : index + 1, :] * owned_ref[
                index, start : start + tall, :
            ].astype(jnp.float32)
        total = total.astype(update_ref.dtype)
        for piece in range(pieces):
            update_ref[piece, start : start + tall, :] = total[
                :, piece * width : (piece + 1) * width
            ]


def finish(parts, neighbours, owned, pieces):
    clients, rows, columns = owned.shape
    vmem = pl.BlockSpec(memory_space=pltpu.VMEM)
    return pl.pallas_call(
        finish_kernel,
        in_specs=[vmem] * 3,
        out_specs=[vmem] * 2,
        out_shape=[
            jax.ShapeDtypeStruct((pieces, rows, columns // pieces), jnp.bfloat16),
            jax.ShapeDtypeStruct((1, clients), jnp.float32),
        ],
        cost_estimate=pl.CostEstimate(
            flops=2 * clients * rows * columns,
            bytes_accessed=2 * clients * rows * columns + 2 * rows * columns,
            transcendentals=clients,
        ),
        name="finish",
    )(parts, neighbours, owned)


def down_kernel(hidden_ref, weight_ref, out_ref):
    out_ref[...] = contract(weight_ref[...], hidden_ref[...], 0, 0).astype(out_ref.dtype)


def project_down(hidden, weight):
    units, tokens = hidden.shape
    features = weight.shape[1]
    chunks = 3
    rows = features // chunks
    return pl.pallas_call(
        down_kernel,
        grid=(chunks,),
        in_specs=[
            pl.BlockSpec((units, tokens), lambda chunk: (0, 0)),
            pl.BlockSpec((units, rows), lambda chunk: (0, chunk)),
        ],
        out_specs=pl.BlockSpec((rows, tokens), lambda chunk: (chunk, 0)),
        out_shape=jax.ShapeDtypeStruct((features, tokens), jnp.bfloat16),
        cost_estimate=pl.CostEstimate(
            flops=2 * units * tokens * features,
            bytes_accessed=2 * (units * features + units * tokens + tokens * features),
            transcendentals=0,
        ),
        name="project_down",
    )(hidden, weight)


def times_kernel(first, last, core_ref, own_ref, other_ref, near_ref, far_ref, out_ref):
    slices, _, depth = own_ref.shape
    step = pl.program_id(0)
    flat = (slices * (last - first), depth)
    total = contract(own_ref[:, first:last, :].reshape(flat), near_ref[...], 1, 0)
    total += contract(other_ref[:, first:last, :].reshape(flat), far_ref[...], 1, 0)
    total = total.reshape(out_ref.shape)

    @pl.when(step == 0)
    def _():
        out_ref[...] = total

    @pl.when(step > 0)
    def _():
        out_ref[...] += total


def times_weights(core, own, other, rows, height, first, last):
    slices, _, depth = own.shape
    tokens = rows.shape[1]
    pieces = other.shape[1] // height
    weight_spec = pl.BlockSpec((slices, height, depth), lambda step, core_ref: (0, step, 0))
    return pl.pallas_call(
        lambda *refs: times_kernel(first, last, *refs),
        grid_spec=pltpu.PrefetchScalarGridSpec(
            num_scalar_prefetch=1,
            grid=(pieces,),
            in_specs=[
                weight_spec,
                weight_spec,
                pl.BlockSpec(
                    (depth, tokens), lambda step, core_ref: (core_ref[0] * pieces + step, 0)
                ),
                pl.BlockSpec(
                    (depth, tokens), lambda step, core_ref: ((1 - core_ref[0]) * pieces + step, 0)
                ),
            ],
            out_specs=pl.BlockSpec(
                (slices, last - first, tokens), lambda step, core_ref: (0, 0, 0)
            ),
        ),
        out_shape=jax.ShapeDtypeStruct((slices, last - first, tokens), jnp.float32),
        cost_estimate=pl.CostEstimate(
            flops=4 * slices * (last - first) * depth * pieces * tokens,
            bytes_accessed=4 * slices * height * depth * pieces + 4 * depth * pieces * tokens,
            transcendentals=0,
        ),
        name="times_weights",
    )(core, own, other, rows, rows)


def delta_kernel(ahead_ref, back_ref, normed_ref, residual_ref, out_ref):
    planes, _, rows, tokens = normed_ref.shape
    slices, ahead_rows, _ = ahead_ref.shape
    back_rows = back_ref.shape[1]
    columns = planes * rows
    shared = ahead_rows + back_rows - out_ref.shape[1]
    ahead = contract(
        ahead_ref[...].reshape(slices * ahead_rows, tokens),
        normed_ref[...].reshape(columns, tokens), 1, 1,
    ).reshape(slices, ahead_rows, columns)
    back = contract(
        back_ref[...].reshape(slices * back_rows, tokens),
        residual_ref[...].reshape(columns, tokens), 1, 1,
    ).reshape(slices, back_rows, columns)
    first = ahead_rows - shared
    out_ref[:, :first, :] = (-ahead[:, :first]).astype(out_ref.dtype)
    both = ahead[:, first:] + back[:, :shared]
    out_ref[:, first:ahead_rows, :] = (-both).astype(out_ref.dtype)
    out_ref[:, ahead_rows:, :] = (-back[:, shared:]).astype(out_ref.dtype)


def make_deltas(ahead, back, normed, residual, height):
    planes, cores, rows, tokens = normed.shape
    slices = ahead.shape[0]
    whole = lambda left: pl.BlockSpec(left.shape, lambda core: (0, 0, 0))
    right_spec = pl.BlockSpec((planes, 1, rows, tokens), lambda core: (0, core, 0, 0))
    return pl.pallas_call(
        delta_kernel,
        grid=(cores,),
        in_specs=[whole(ahead), whole(back), right_spec, right_spec],
        out_specs=pl.BlockSpec((slices, height, planes * rows), lambda core: (core, 0, 0)),
        out_shape=jax.ShapeDtypeStruct((cores * slices, height, planes * rows), jnp.bfloat16),
        cost_estimate=pl.CostEstimate(
            flops=2 * slices * (ahead.shape[1] + back.shape[1]) * planes * cores * rows * tokens,
            bytes_accessed=4 * planes * cores * rows * tokens
            + 2 * slices * height * planes * cores * rows,
            transcendentals=0,
        ),
        name="make_deltas",
    )(ahead, back, normed, residual)


def rms_normed(raw, norm_gain):
    widened = raw.astype(jnp.float32)
    inverse_rms = lax.rsqrt(jnp.mean(widened * widened, axis=0, keepdims=True) + 1e-06)
    return (widened * inverse_rms * norm_gain[:, None]).astype(jnp.bfloat16)


def swap_blocks(shard, z_count, core_count):
    pairs = [
        ((z * core_count + core) * z_count + p, (p * core_count + core) * z_count + z)
        for z in range(z_count)
        for core in range(core_count)
        for p in range(z_count)
    ]
    return lax.ppermute(shard, ZC + XY, pairs)


def on_device(inputs, targets, norm_gain, gate_weight, up_weight, down_weight, neighbours):
    token_count = inputs.shape[1]
    param_count = lax.axis_size(XY)
    z_count = lax.axis_size("z")
    core_count = lax.axis_size("core")
    client_count = z_count * core_count
    factor = 1.0 / math.sqrt(token_count)
    features = param_count * inputs.shape[2]
    slice_rows = features // client_count
    hidden_units = gate_weight.shape[1]

    own_inputs = inputs[0].T
    met_inputs = lax.all_gather(own_inputs, "z", axis=0, tiled=False)
    gathered = gather_rows(own_inputs, XY, param_count)
    normed = rms_normed(gathered, norm_gain)
    gate_value = contract(gate_weight, normed, 0, 0)
    up_value = contract(up_weight, normed, 0, 0)
    hidden = (gelu_tanh(gate_value) * up_value).astype(jnp.bfloat16)
    partial_out = project_down(hidden, down_weight)
    parts = exchange(
        partial_out.reshape(param_count, features // param_count, token_count), XY
    )
    summed = jnp.sum(parts.astype(jnp.float32), axis=0)
    own_residual = ((summed - targets[0].T.astype(jnp.float32)) * factor).astype(jnp.bfloat16)
    met_residual = swap_blocks(own_residual, z_count, core_count)
    met_residual = lax.all_gather(met_residual, "z", axis=0, tiled=True)

    share = hidden_units // z_count
    height = -(-3 * share // 8) * 8
    first = lax.axis_index("z") * share
    column = lax.axis_index("core") * (features // core_count)

    def own_part(rows):
        return lax.dynamic_slice(rows, (first, column), (share, features // core_count))

    ahead_rows = -(-2 * share // 8) * 8
    back_rows = -(-share // 8) * 8

    def fill(rows):
        return jnp.zeros((rows, features // core_count), jnp.bfloat16)

    part = jnp.concatenate(
        [
            own_part(gate_weight.T),
            own_part(up_weight.T),
            fill(ahead_rows - 2 * share),
            own_part(down_weight),
            fill(back_rows - share),
        ],
        axis=0,
    )
    weight_rows = ahead_rows + back_rows
    pieces = features // core_count // token_count
    part = jnp.concatenate(jnp.split(part, pieces, axis=1), axis=0)
    part, met_inputs, own_residual = lax.optimization_barrier((part, met_inputs, own_residual))
    copies = jnp.broadcast_to(part[None], (param_count,) + part.shape)
    both = exchange(jnp.concatenate([copies, met_inputs], axis=1), XY)
    met_inputs = both[:, pieces * weight_rows :].reshape(features, token_count)
    part = both[:, : pieces * weight_rows]
    other = lax.ppermute(part, "core", [(0, 1), (1, 0)])
    core = lax.axis_index("core").reshape(1)
    met_normed = rms_normed(met_inputs, norm_gain)
    values = times_weights(core, both, other, met_normed, weight_rows, 0, ahead_rows)
    values, met_residual = lax.optimization_barrier((values, met_residual))
    activated, gelu_back = jax.vjp(gelu_tanh, values[:, :share])
    up_value = values[:, share : 2 * share]
    hidden = (activated * up_value).astype(jnp.bfloat16)
    back_hidden = times_weights(
        core, both, other, met_residual, weight_rows, ahead_rows, weight_rows
    )[:, :share]
    back_gate = gelu_back(back_hidden * up_value)[0].astype(jnp.bfloat16)
    back_up = (back_hidden * activated).astype(jnp.bfloat16)

    def blank(rows):
        return jnp.zeros((param_count, rows, token_count), jnp.bfloat16)

    lead = 2 * share - (height - back_rows)
    by_plane = (z_count, core_count, slice_rows, token_count)
    deltas = make_deltas(
        jnp.concatenate([back_gate, back_up, blank(ahead_rows - 2 * share)], axis=1),
        jnp.concatenate([blank(lead), hidden, blank(back_rows - share - lead)], axis=1),
        met_normed.reshape(by_plane),
        met_residual.reshape(by_plane),
        height,
    )
    owned = exchange(deltas, ("core",) + XY)

    gram = pair_products(owned, core_count * param_count)
    gram = jnp.sum(exchange(gram, ("core",) + XY), axis=0)
    gram = exchange(jnp.broadcast_to(gram[None], (z_count,) + gram.shape), "z")
    order = neighbours.reshape(z_count, core_count).T.reshape(1, -1)
    update, relative = finish(gram, order, owned, z_count)
    update = exchange(update, "z").astype(jnp.float32)

    def placed(index):
        rows = update[:, index * share : (index + 1) * share]
        return rows.reshape(hidden_units, slice_rows).T

    return (
        placed(0),
        placed(1),
        placed(2),
        relative.reshape(core_count, z_count).T.reshape(-1),
    )


def solution(mesh):
    torus = Mesh(mesh.devices.reshape(16, 2, 4, 4), ("z", "core", "x", "y"))
    in_specs = (
        P(ZC, None, XY),
        P(ZC, None, XY),
        P(),
        P(None, XY),
        P(None, XY),
        P(XY, None),
        P(),
    )
    out_specs = (P(ZC, XY), P(ZC, XY), P(ZC, XY), P())
    return jax.shard_map(
        on_device, mesh=torus, in_specs=in_specs, out_specs=out_specs, check_vma=False
    )
```

```python
import math

import jax
import jax.numpy as jnp
from jax import lax
from jax.experimental import pallas as pl
from jax.experimental.pallas import tpu as pltpu
from jax.sharding import Mesh, PartitionSpec as P


XY = ("x", "y")
ZC = ("z", "core")


def gelu_tanh(values):
    return jax.nn.gelu(values, approximate=True)


def exchange(blocks, axes):
    return lax.all_to_all(blocks, axes, split_axis=0, concat_axis=0, tiled=True)


def gather_rows(shard, axes, count):
    copies = jnp.broadcast_to(shard[None], (count,) + shard.shape)
    return exchange(copies, axes).reshape((count * shard.shape[0],) + shard.shape[1:])


def contract(left, right, left_dim, right_dim):
    return lax.dot_general(
        left, right, (((left_dim,), (right_dim,)), ((), ())), preferred_element_type=jnp.float32
    )


def exact_dot(left, right, left_dim, right_dim):
    return lax.dot_general(
        left, right, (((left_dim,), (right_dim,)), ((), ())),
        precision=lax.Precision.HIGHEST, preferred_element_type=jnp.float32,
    )


def lane_place(index, size, lanes):
    row = lax.broadcasted_iota(jnp.int32, (size, lanes), 0)
    column = lax.broadcasted_iota(jnp.int32, (size, lanes), 1)
    return (column == row + index * size).astype(jnp.float32)


def gram_kernel(block_ref, copies_ref, total_ref):
    clients, tall, columns = block_ref.shape
    size = clients * tall
    step = pl.program_id(0)
    tile = block_ref[...].reshape(size, columns)

    @pl.when(step == 0)
    def _():
        total_ref[...] = jnp.zeros_like(total_ref)

    total_ref[...] += contract(tile, tile, 1, 1)

    @pl.when(step == pl.num_programs(0) - 1)
    def _():
        row_index = lax.broadcasted_iota(jnp.int32, (size, size), 0)
        col_index = lax.broadcasted_iota(jnp.int32, (size, size), 1)
        kept = jnp.where(row_index % tall == col_index % tall, total_ref[...], 0.0)
        pick_client = lax.broadcasted_iota(jnp.int32, (clients, size), 0)
        pick_row = lax.broadcasted_iota(jnp.int32, (clients, size), 1) // tall
        pick = (pick_row == pick_client).astype(jnp.float32)
        gram = exact_dot(exact_dot(pick, kept, 1, 0), pick, 1, 1)
        packed = jnp.zeros(copies_ref.shape[1:], jnp.float32)
        for index in range(clients // tall):
            packed += exact_dot(
                gram[index * tall : (index + 1) * tall],
                lane_place(index, clients, copies_ref.shape[2]), 1, 0,
            )
        copies_ref[...] = jnp.broadcast_to(packed[None], copies_ref.shape)


def pair_products(exchanged, copies):
    clients, rows, columns = exchanged.shape
    tall = 8
    return pl.pallas_call(
        gram_kernel,
        grid=(rows // tall,),
        in_specs=[pl.BlockSpec((clients, tall, columns), lambda step: (0, step, 0))],
        out_specs=pl.BlockSpec((copies, 8, 128), lambda step: (0, 0, 0)),
        out_shape=jax.ShapeDtypeStruct((copies, 8, 128), jnp.float32),
        scratch_shapes=[pltpu.VMEM((clients * tall, clients * tall), jnp.float32)],
        cost_estimate=pl.CostEstimate(
            flops=2 * rows * clients * clients * tall * columns,
            bytes_accessed=2 * clients * rows * columns,
            transcendentals=0,
        ),
        name="pair_products",
    )(exchanged)


def finish_kernel(parts_ref, neighbours_ref, owned_ref, update_ref, relative_ref):
    clients, rows, columns = owned_ref.shape
    pieces, _, width = update_ref.shape
    tall = 8
    packed = jnp.sum(parts_ref[...], axis=0)
    gram = jnp.concatenate(
        [
            exact_dot(packed, lane_place(index, clients, packed.shape[1]), 1, 1)
            for index in range(clients // tall)
        ],
        axis=0,
    )
    row_index = lax.broadcasted_iota(jnp.int32, (clients, clients), 0)
    col_index = lax.broadcasted_iota(jnp.int32, (clients, clients), 1)
    same = row_index == col_index
    diagonal = jnp.where(same, gram, 0.0)
    distance = (
        jnp.sum(diagonal, axis=1, keepdims=True)
        + jnp.sum(diagonal, axis=0, keepdims=True)
        - 2.0 * gram
    )
    distance = jnp.where(same, 1e30, distance)
    rank = jnp.zeros((clients, clients), jnp.float32)
    for index in range(clients):
        rival = distance[:, index : index + 1]
        ahead = (rival < distance) | ((rival == distance) & (index < col_index))
        rank += jnp.where(ahead, 1.0, 0.0)
    count = jnp.sum(
        jnp.where(same, neighbours_ref[...].astype(jnp.float32), 0.0), axis=1, keepdims=True
    )
    scores = jnp.sum(jnp.where(rank < count, distance, 0.0), axis=1, keepdims=True)
    mean = jnp.sum(scores, axis=0, keepdims=True) / clients
    exponent = jnp.exp(-4.0 * (scores / mean))
    weights = exponent / jnp.sum(exponent, axis=0, keepdims=True)
    relative_ref[...] = clients * jnp.sum(jnp.where(same, weights, 0.0), axis=0, keepdims=True)
    for start in range(0, rows, tall):
        total = jnp.zeros((tall, columns), jnp.float32)
        for index in range(clients):
            total += weights[index : index + 1, :] * owned_ref[
                index, start : start + tall, :
            ].astype(jnp.float32)
        total = total.astype(update_ref.dtype)
        for piece in range(pieces):
            update_ref[piece, start : start + tall, :] = total[
                :, piece * width : (piece + 1) * width
            ]


def finish(parts, neighbours, owned, pieces):
    clients, rows, columns = owned.shape
    vmem = pl.BlockSpec(memory_space=pltpu.VMEM)
    return pl.pallas_call(
        finish_kernel,
        in_specs=[vmem] * 3,
        out_specs=[vmem] * 2,
        out_shape=[
            jax.ShapeDtypeStruct((pieces, rows, columns // pieces), jnp.bfloat16),
            jax.ShapeDtypeStruct((1, clients), jnp.float32),
        ],
        cost_estimate=pl.CostEstimate(
            flops=2 * clients * rows * columns,
            bytes_accessed=2 * clients * rows * columns + 2 * rows * columns,
            transcendentals=clients,
        ),
        name="finish",
    )(parts, neighbours, owned)


def down_kernel(hidden_ref, weight_ref, out_ref):
    out_ref[...] = contract(weight_ref[...], hidden_ref[...], 0, 0).astype(out_ref.dtype)


def project_down(hidden, weight):
    units, tokens = hidden.shape
    features = weight.shape[1]
    chunks = 3
    rows = features // chunks
    return pl.pallas_call(
        down_kernel,
        grid=(chunks,),
        in_specs=[
            pl.BlockSpec((units, tokens), lambda chunk: (0, 0)),
            pl.BlockSpec((units, rows), lambda chunk: (0, chunk)),
        ],
        out_specs=pl.BlockSpec((rows, tokens), lambda chunk: (chunk, 0)),
        out_shape=jax.ShapeDtypeStruct((features, tokens), jnp.bfloat16),
        cost_estimate=pl.CostEstimate(
            flops=2 * units * tokens * features,
            bytes_accessed=2 * (units * features + units * tokens + tokens * features),
            transcendentals=0,
        ),
        name="project_down",
    )(hidden, weight)


def times_kernel(core_ref, own_ref, other_ref, near_ref, far_ref, out_ref):
    slices, height, depth = own_ref.shape
    step = pl.program_id(0)
    flat = (slices * height, depth)
    total = contract(own_ref[...].reshape(flat), near_ref[...], 1, 0)
    total += contract(other_ref[...].reshape(flat), far_ref[...], 1, 0)
    total = total.reshape(out_ref.shape)

    @pl.when(step == 0)
    def _():
        out_ref[...] = total

    @pl.when(step > 0)
    def _():
        out_ref[...] += total


def times_weights(core, own, other, rows, pieces, start, height):
    slices, _, depth = own.shape
    tokens = rows.shape[1]
    if start % height:
        raise ValueError("unaligned pieces")
    first = start // height
    weight_spec = pl.BlockSpec((slices, height, depth), lambda step, core_ref: (0, first + step, 0))
    return pl.pallas_call(
        times_kernel,
        grid_spec=pltpu.PrefetchScalarGridSpec(
            num_scalar_prefetch=1,
            grid=(pieces,),
            in_specs=[
                weight_spec,
                weight_spec,
                pl.BlockSpec(
                    (depth, tokens), lambda step, core_ref: (core_ref[0] * pieces + step, 0)
                ),
                pl.BlockSpec(
                    (depth, tokens), lambda step, core_ref: ((1 - core_ref[0]) * pieces + step, 0)
                ),
            ],
            out_specs=pl.BlockSpec((slices, height, tokens), lambda step, core_ref: (0, 0, 0)),
        ),
        out_shape=jax.ShapeDtypeStruct((slices, height, tokens), jnp.float32),
        cost_estimate=pl.CostEstimate(
            flops=4 * slices * height * depth * pieces * tokens,
            bytes_accessed=4 * slices * height * depth * pieces + 4 * depth * pieces * tokens,
            transcendentals=0,
        ),
        name="times_weights",
    )(core, own, other, rows, rows)


def delta_kernel(ahead_ref, back_ref, normed_ref, residual_ref, out_ref):
    planes, _, rows, tokens = normed_ref.shape
    slices, ahead_rows, _ = ahead_ref.shape
    back_rows = back_ref.shape[1]
    columns = planes * rows
    shared = ahead_rows + back_rows - out_ref.shape[1]
    ahead = contract(
        ahead_ref[...].reshape(slices * ahead_rows, tokens),
        normed_ref[...].reshape(columns, tokens), 1, 1,
    ).reshape(slices, ahead_rows, columns)
    back = contract(
        back_ref[...].reshape(slices * back_rows, tokens),
        residual_ref[...].reshape(columns, tokens), 1, 1,
    ).reshape(slices, back_rows, columns)
    first = ahead_rows - shared
    out_ref[:, :first, :] = (-ahead[:, :first]).astype(out_ref.dtype)
    both = ahead[:, first:] + back[:, :shared]
    out_ref[:, first:ahead_rows, :] = (-both).astype(out_ref.dtype)
    out_ref[:, ahead_rows:, :] = (-back[:, shared:]).astype(out_ref.dtype)


def make_deltas(ahead, back, normed, residual, height):
    planes, cores, rows, tokens = normed.shape
    slices = ahead.shape[0]
    whole = lambda left: pl.BlockSpec(left.shape, lambda core: (0, 0, 0))
    right_spec = pl.BlockSpec((planes, 1, rows, tokens), lambda core: (0, core, 0, 0))
    return pl.pallas_call(
        delta_kernel,
        grid=(cores,),
        in_specs=[whole(ahead), whole(back), right_spec, right_spec],
        out_specs=pl.BlockSpec((slices, height, planes * rows), lambda core: (core, 0, 0)),
        out_shape=jax.ShapeDtypeStruct((cores * slices, height, planes * rows), jnp.bfloat16),
        cost_estimate=pl.CostEstimate(
            flops=2 * slices * (ahead.shape[1] + back.shape[1]) * planes * cores * rows * tokens,
            bytes_accessed=4 * planes * cores * rows * tokens
            + 2 * slices * height * planes * cores * rows,
            transcendentals=0,
        ),
        name="make_deltas",
    )(ahead, back, normed, residual)


def rms_normed(raw, norm_gain):
    widened = raw.astype(jnp.float32)
    inverse_rms = lax.rsqrt(jnp.mean(widened * widened, axis=0, keepdims=True) + 1e-06)
    return (widened * inverse_rms * norm_gain[:, None]).astype(jnp.bfloat16)


def swap_blocks(shard, z_count, core_count):
    pairs = [
        ((z * core_count + core) * z_count + p, (p * core_count + core) * z_count + z)
        for z in range(z_count)
        for core in range(core_count)
        for p in range(z_count)
    ]
    return lax.ppermute(shard, ZC + XY, pairs)


def on_device(inputs, targets, norm_gain, gate_weight, up_weight, down_weight, neighbours):
    token_count = inputs.shape[1]
    param_count = lax.axis_size(XY)
    z_count = lax.axis_size("z")
    core_count = lax.axis_size("core")
    client_count = z_count * core_count
    factor = 1.0 / math.sqrt(token_count)
    features = param_count * inputs.shape[2]
    slice_rows = features // client_count
    hidden_units = gate_weight.shape[1]

    own_inputs = inputs[0].T
    met_inputs = lax.all_gather(own_inputs, "z", axis=0, tiled=False)
    gathered = gather_rows(own_inputs, XY, param_count)
    normed = rms_normed(gathered, norm_gain)
    gate_value = contract(gate_weight, normed, 0, 0)
    up_value = contract(up_weight, normed, 0, 0)
    hidden = (gelu_tanh(gate_value) * up_value).astype(jnp.bfloat16)
    partial_out = project_down(hidden, down_weight)
    parts = exchange(
        partial_out.reshape(param_count, features // param_count, token_count), XY
    )
    summed = jnp.sum(parts.astype(jnp.float32), axis=0)
    own_residual = ((summed - targets[0].T.astype(jnp.float32)) * factor).astype(jnp.bfloat16)
    met_residual = swap_blocks(own_residual, z_count, core_count)
    met_residual = lax.all_gather(met_residual, "z", axis=0, tiled=True)

    share = hidden_units // z_count
    height = -(-3 * share // 8) * 8
    first = lax.axis_index("z") * share
    column = lax.axis_index("core") * (features // core_count)

    def own_part(rows):
        return lax.dynamic_slice(rows, (first, column), (share, features // core_count))

    ahead_rows = -(-2 * share // 8) * 8
    back_rows = -(-share // 8) * 8

    def fill(rows):
        return jnp.zeros((rows, features // core_count), jnp.bfloat16)

    part = jnp.concatenate(
        [
            own_part(gate_weight.T),
            own_part(up_weight.T),
            fill(ahead_rows - 2 * share),
            own_part(down_weight),
            fill(back_rows - share),
        ],
        axis=0,
    )
    weight_rows = ahead_rows + back_rows
    pieces = features // core_count // token_count
    part = jnp.concatenate(
        jnp.split(part[:ahead_rows], pieces, axis=1) + jnp.split(part[ahead_rows:], pieces, axis=1),
        axis=0,
    )
    part, met_inputs, own_residual = lax.optimization_barrier((part, met_inputs, own_residual))
    copies = jnp.broadcast_to(part[None], (param_count,) + part.shape)
    both = exchange(jnp.concatenate([copies, met_inputs], axis=1), XY)
    met_inputs = both[:, pieces * weight_rows :].reshape(features, token_count)
    part = both[:, : pieces * weight_rows]
    other = lax.ppermute(part, "core", [(0, 1), (1, 0)])
    core = lax.axis_index("core").reshape(1)
    met_normed = rms_normed(met_inputs, norm_gain)
    values = times_weights(core, both, other, met_normed, pieces, 0, ahead_rows)
    values, met_residual = lax.optimization_barrier((values, met_residual))
    activated, gelu_back = jax.vjp(gelu_tanh, values[:, :share])
    up_value = values[:, share : 2 * share]
    hidden = (activated * up_value).astype(jnp.bfloat16)
    back_hidden = times_weights(
        core, both, other, met_residual, pieces, pieces * ahead_rows, back_rows
    )[:, :share]
    back_gate = gelu_back(back_hidden * up_value)[0].astype(jnp.bfloat16)
    back_up = (back_hidden * activated).astype(jnp.bfloat16)

    def blank(rows):
        return jnp.zeros((param_count, rows, token_count), jnp.bfloat16)

    lead = 2 * share - (height - back_rows)
    by_plane = (z_count, core_count, slice_rows, token_count)
    deltas = make_deltas(
        jnp.concatenate([back_gate, back_up, blank(ahead_rows - 2 * share)], axis=1),
        jnp.concatenate([blank(lead), hidden, blank(back_rows - share - lead)], axis=1),
        met_normed.reshape(by_plane),
        met_residual.reshape(by_plane),
        height,
    )
    owned = exchange(deltas, ("core",) + XY)

    gram = pair_products(owned, core_count * param_count)
    gram = jnp.sum(exchange(gram, ("core",) + XY), axis=0)
    gram = exchange(jnp.broadcast_to(gram[None], (z_count,) + gram.shape), "z")
    order = neighbours.reshape(z_count, core_count).T.reshape(1, -1)
    update, relative = finish(gram, order, owned, z_count)
    update = exchange(update, "z").astype(jnp.float32)

    def placed(index):
        rows = update[:, index * share : (index + 1) * share]
        return rows.reshape(hidden_units, slice_rows).T

    return (
        placed(0),
        placed(1),
        placed(2),
        relative.reshape(core_count, z_count).T.reshape(-1),
    )


def solution(mesh):
    torus = Mesh(mesh.devices.reshape(16, 2, 4, 4), ("z", "core", "x", "y"))
    in_specs = (
        P(ZC, None, XY),
        P(ZC, None, XY),
        P(),
        P(None, XY),
        P(None, XY),
        P(XY, None),
        P(),
    )
    out_specs = (P(ZC, XY), P(ZC, XY), P(ZC, XY), P())
    return jax.shard_map(
        on_device, mesh=torus, in_specs=in_specs, out_specs=out_specs, check_vma=False
    )
```

```python
import math

import jax
import jax.numpy as jnp
from jax import lax
from jax.experimental import pallas as pl
from jax.experimental.pallas import tpu as pltpu
from jax.sharding import Mesh, PartitionSpec as P


XY = ("x", "y")
ZC = ("z", "core")


def gelu_tanh(values):
    return jax.nn.gelu(values, approximate=True)


def exchange(blocks, axes):
    return lax.all_to_all(blocks, axes, split_axis=0, concat_axis=0, tiled=True)


def gather_rows(shard, axes, count):
    copies = jnp.broadcast_to(shard[None], (count,) + shard.shape)
    return exchange(copies, axes).reshape((count * shard.shape[0],) + shard.shape[1:])


def contract(left, right, left_dim, right_dim):
    return lax.dot_general(
        left, right, (((left_dim,), (right_dim,)), ((), ())), preferred_element_type=jnp.float32
    )


def exact_dot(left, right, left_dim, right_dim):
    return lax.dot_general(
        left, right, (((left_dim,), (right_dim,)), ((), ())),
        precision=lax.Precision.HIGHEST, preferred_element_type=jnp.float32,
    )


def lane_place(index, size, lanes):
    row = lax.broadcasted_iota(jnp.int32, (size, lanes), 0)
    column = lax.broadcasted_iota(jnp.int32, (size, lanes), 1)
    return (column == row + index * size).astype(jnp.float32)


def gram_kernel(block_ref, copies_ref, total_ref):
    clients, rows, columns = block_ref.shape
    tall = 8
    size = clients * tall
    total_ref[...] = jnp.zeros_like(total_ref)

    @pl.loop(0, rows // tall)
    def _(index):
        start = pl.multiple_of(index * tall, tall)
        tile = block_ref[:, pl.ds(start, tall), :].reshape(size, columns)
        total_ref[...] += contract(tile, tile, 1, 1)

    row_index = lax.broadcasted_iota(jnp.int32, (size, size), 0)
    col_index = lax.broadcasted_iota(jnp.int32, (size, size), 1)
    kept = jnp.where(row_index % tall == col_index % tall, total_ref[...], 0.0)
    pick_client = lax.broadcasted_iota(jnp.int32, (clients, size), 0)
    pick_row = lax.broadcasted_iota(jnp.int32, (clients, size), 1) // tall
    pick = (pick_row == pick_client).astype(jnp.float32)
    gram = exact_dot(exact_dot(pick, kept, 1, 0), pick, 1, 1)
    packed = jnp.zeros(copies_ref.shape[1:], jnp.float32)
    for index in range(clients // tall):
        packed += exact_dot(
            gram[index * tall : (index + 1) * tall],
            lane_place(index, clients, copies_ref.shape[2]), 1, 0,
        )
    copies_ref[...] = jnp.broadcast_to(packed[None], copies_ref.shape)


def pair_products(exchanged, copies):
    clients, rows, columns = exchanged.shape
    return pl.pallas_call(
        gram_kernel,
        out_shape=jax.ShapeDtypeStruct((copies, 8, 128), jnp.float32),
        in_specs=[pl.BlockSpec(memory_space=pltpu.VMEM)],
        out_specs=pl.BlockSpec(memory_space=pltpu.VMEM),
        scratch_shapes=[pltpu.VMEM((clients * 8, clients * 8), jnp.float32)],
        cost_estimate=pl.CostEstimate(
            flops=2 * rows * clients * clients * 8 * columns,
            bytes_accessed=2 * clients * rows * columns,
            transcendentals=0,
        ),
        name="pair_products",
    )(exchanged)


def finish_kernel(parts_ref, neighbours_ref, owned_ref, update_ref, relative_ref):
    clients, rows, columns = owned_ref.shape
    pieces, _, width = update_ref.shape
    tall = 8
    packed = jnp.sum(parts_ref[...], axis=0)
    gram = jnp.concatenate(
        [
            exact_dot(packed, lane_place(index, clients, packed.shape[1]), 1, 1)
            for index in range(clients // tall)
        ],
        axis=0,
    )
    row_index = lax.broadcasted_iota(jnp.int32, (clients, clients), 0)
    col_index = lax.broadcasted_iota(jnp.int32, (clients, clients), 1)
    same = row_index == col_index
    diagonal = jnp.where(same, gram, 0.0)
    distance = (
        jnp.sum(diagonal, axis=1, keepdims=True)
        + jnp.sum(diagonal, axis=0, keepdims=True)
        - 2.0 * gram
    )
    distance = jnp.where(same, 1e30, distance)
    rank = jnp.zeros((clients, clients), jnp.float32)
    for index in range(clients):
        rival = distance[:, index : index + 1]
        ahead = (rival < distance) | ((rival == distance) & (index < col_index))
        rank += jnp.where(ahead, 1.0, 0.0)
    count = jnp.sum(
        jnp.where(same, neighbours_ref[...].astype(jnp.float32), 0.0), axis=1, keepdims=True
    )
    scores = jnp.sum(jnp.where(rank < count, distance, 0.0), axis=1, keepdims=True)
    mean = jnp.sum(scores, axis=0, keepdims=True) / clients
    exponent = jnp.exp(-4.0 * (scores / mean))
    weights = exponent / jnp.sum(exponent, axis=0, keepdims=True)
    relative_ref[...] = clients * jnp.sum(jnp.where(same, weights, 0.0), axis=0, keepdims=True)
    for start in range(0, rows, tall):
        total = jnp.zeros((tall, columns), jnp.float32)
        for index in range(clients):
            total += weights[index : index + 1, :] * owned_ref[
                index, start : start + tall, :
            ].astype(jnp.float32)
        total = total.astype(update_ref.dtype)
        for piece in range(pieces):
            update_ref[piece, start : start + tall, :] = total[
                :, piece * width : (piece + 1) * width
            ]


def finish(parts, neighbours, owned, pieces):
    clients, rows, columns = owned.shape
    vmem = pl.BlockSpec(memory_space=pltpu.VMEM)
    return pl.pallas_call(
        finish_kernel,
        in_specs=[vmem] * 3,
        out_specs=[vmem] * 2,
        out_shape=[
            jax.ShapeDtypeStruct((pieces, rows, columns // pieces), jnp.bfloat16),
            jax.ShapeDtypeStruct((1, clients), jnp.float32),
        ],
        cost_estimate=pl.CostEstimate(
            flops=2 * clients * rows * columns,
            bytes_accessed=2 * clients * rows * columns + 2 * rows * columns,
            transcendentals=clients,
        ),
        name="finish",
    )(parts, neighbours, owned)


def down_kernel(hidden_ref, weight_ref, out_ref):
    out_ref[...] = contract(weight_ref[...], hidden_ref[...], 0, 0).astype(out_ref.dtype)


def project_down(hidden, weight):
    units, tokens = hidden.shape
    features = weight.shape[1]
    chunks = 3
    rows = features // chunks
    return pl.pallas_call(
        down_kernel,
        grid=(chunks,),
        in_specs=[
            pl.BlockSpec((units, tokens), lambda chunk: (0, 0)),
            pl.BlockSpec((units, rows), lambda chunk: (0, chunk)),
        ],
        out_specs=pl.BlockSpec((rows, tokens), lambda chunk: (chunk, 0)),
        out_shape=jax.ShapeDtypeStruct((features, tokens), jnp.bfloat16),
        cost_estimate=pl.CostEstimate(
            flops=2 * units * tokens * features,
            bytes_accessed=2 * (units * features + units * tokens + tokens * features),
            transcendentals=0,
        ),
        name="project_down",
    )(hidden, weight)


def times_kernel(core_ref, own_ref, other_ref, near_ref, far_ref, out_ref):
    slices, height, depth = own_ref.shape
    step = pl.program_id(0)
    flat = (slices * height, depth)
    total = contract(own_ref[...].reshape(flat), near_ref[...], 1, 0)
    total += contract(other_ref[...].reshape(flat), far_ref[...], 1, 0)
    total = total.reshape(out_ref.shape)

    @pl.when(step == 0)
    def _():
        out_ref[...] = total

    @pl.when(step > 0)
    def _():
        out_ref[...] += total


def times_weights(core, own, other, rows, pieces, start, height):
    slices, _, depth = own.shape
    tokens = rows.shape[1]
    if start % height:
        raise ValueError("unaligned pieces")
    first = start // height
    weight_spec = pl.BlockSpec((slices, height, depth), lambda step, core_ref: (0, first + step, 0))
    return pl.pallas_call(
        times_kernel,
        grid_spec=pltpu.PrefetchScalarGridSpec(
            num_scalar_prefetch=1,
            grid=(pieces,),
            in_specs=[
                weight_spec,
                weight_spec,
                pl.BlockSpec(
                    (depth, tokens), lambda step, core_ref: (core_ref[0] * pieces + step, 0)
                ),
                pl.BlockSpec(
                    (depth, tokens), lambda step, core_ref: ((1 - core_ref[0]) * pieces + step, 0)
                ),
            ],
            out_specs=pl.BlockSpec((slices, height, tokens), lambda step, core_ref: (0, 0, 0)),
        ),
        out_shape=jax.ShapeDtypeStruct((slices, height, tokens), jnp.float32),
        cost_estimate=pl.CostEstimate(
            flops=4 * slices * height * depth * pieces * tokens,
            bytes_accessed=4 * slices * height * depth * pieces + 4 * depth * pieces * tokens,
            transcendentals=0,
        ),
        name="times_weights",
    )(core, own, other, rows, rows)


def delta_kernel(ahead_ref, back_ref, normed_ref, residual_ref, out_ref):
    planes, _, rows, tokens = normed_ref.shape
    slices, ahead_rows, _ = ahead_ref.shape
    back_rows = back_ref.shape[1]
    columns = planes * rows
    shared = ahead_rows + back_rows - out_ref.shape[1]
    ahead = contract(
        ahead_ref[...].reshape(slices * ahead_rows, tokens),
        normed_ref[...].reshape(columns, tokens), 1, 1,
    ).reshape(slices, ahead_rows, columns)
    back = contract(
        back_ref[...].reshape(slices * back_rows, tokens),
        residual_ref[...].reshape(columns, tokens), 1, 1,
    ).reshape(slices, back_rows, columns)
    first = ahead_rows - shared
    out_ref[:, :first, :] = (-ahead[:, :first]).astype(out_ref.dtype)
    both = ahead[:, first:] + back[:, :shared]
    out_ref[:, first:ahead_rows, :] = (-both).astype(out_ref.dtype)
    out_ref[:, ahead_rows:, :] = (-back[:, shared:]).astype(out_ref.dtype)


def make_deltas(ahead, back, normed, residual, height):
    planes, cores, rows, tokens = normed.shape
    slices = ahead.shape[0]
    whole = lambda left: pl.BlockSpec(left.shape, lambda core: (0, 0, 0))
    right_spec = pl.BlockSpec((planes, 1, rows, tokens), lambda core: (0, core, 0, 0))
    return pl.pallas_call(
        delta_kernel,
        grid=(cores,),
        in_specs=[whole(ahead), whole(back), right_spec, right_spec],
        out_specs=pl.BlockSpec((slices, height, planes * rows), lambda core: (core, 0, 0)),
        out_shape=jax.ShapeDtypeStruct((cores * slices, height, planes * rows), jnp.bfloat16),
        cost_estimate=pl.CostEstimate(
            flops=2 * slices * (ahead.shape[1] + back.shape[1]) * planes * cores * rows * tokens,
            bytes_accessed=4 * planes * cores * rows * tokens
            + 2 * slices * height * planes * cores * rows,
            transcendentals=0,
        ),
        name="make_deltas",
    )(ahead, back, normed, residual)


def rms_normed(raw, norm_gain):
    widened = raw.astype(jnp.float32)
    inverse_rms = lax.rsqrt(jnp.mean(widened * widened, axis=0, keepdims=True) + 1e-06)
    return (widened * inverse_rms * norm_gain[:, None]).astype(jnp.bfloat16)


def swap_blocks(shard, z_count, core_count):
    pairs = [
        ((z * core_count + core) * z_count + p, (p * core_count + core) * z_count + z)
        for z in range(z_count)
        for core in range(core_count)
        for p in range(z_count)
    ]
    return lax.ppermute(shard, ZC + XY, pairs)


def on_device(inputs, targets, norm_gain, gate_weight, up_weight, down_weight, neighbours):
    token_count = inputs.shape[1]
    param_count = lax.axis_size(XY)
    z_count = lax.axis_size("z")
    core_count = lax.axis_size("core")
    client_count = z_count * core_count
    factor = 1.0 / math.sqrt(token_count)
    features = param_count * inputs.shape[2]
    slice_rows = features // client_count
    hidden_units = gate_weight.shape[1]

    own_inputs = inputs[0].T
    met_inputs = lax.all_gather(own_inputs, "z", axis=0, tiled=False)
    gathered = gather_rows(own_inputs, XY, param_count)
    normed = rms_normed(gathered, norm_gain)
    gate_value = contract(gate_weight, normed, 0, 0)
    up_value = contract(up_weight, normed, 0, 0)
    hidden = (gelu_tanh(gate_value) * up_value).astype(jnp.bfloat16)
    partial_out = project_down(hidden, down_weight)
    parts = exchange(
        partial_out.reshape(param_count, features // param_count, token_count), XY
    )
    summed = jnp.sum(parts.astype(jnp.float32), axis=0)
    own_residual = ((summed - targets[0].T.astype(jnp.float32)) * factor).astype(jnp.bfloat16)
    met_residual = swap_blocks(own_residual, z_count, core_count)
    met_residual = lax.all_gather(met_residual, "z", axis=0, tiled=True)

    share = hidden_units // z_count
    height = -(-3 * share // 8) * 8
    first = lax.axis_index("z") * share
    column = lax.axis_index("core") * (features // core_count)

    def own_part(rows):
        return lax.dynamic_slice(rows, (first, column), (share, features // core_count))

    ahead_rows = -(-2 * share // 8) * 8
    back_rows = -(-share // 8) * 8

    def fill(rows):
        return jnp.zeros((rows, features // core_count), jnp.bfloat16)

    part = jnp.concatenate(
        [
            own_part(gate_weight.T),
            own_part(up_weight.T),
            fill(ahead_rows - 2 * share),
            own_part(down_weight),
            fill(back_rows - share),
        ],
        axis=0,
    )
    weight_rows = ahead_rows + back_rows
    pieces = features // core_count // token_count
    part = jnp.concatenate(
        jnp.split(part[:ahead_rows], pieces, axis=1) + jnp.split(part[ahead_rows:], pieces, axis=1),
        axis=0,
    )
    part, met_inputs, own_residual = lax.optimization_barrier((part, met_inputs, own_residual))
    copies = jnp.broadcast_to(part[None], (param_count,) + part.shape)
    both = exchange(jnp.concatenate([copies, met_inputs], axis=1), XY)
    met_inputs = both[:, pieces * weight_rows :].reshape(features, token_count)
    part = both[:, : pieces * weight_rows]
    other = lax.ppermute(part, "core", [(0, 1), (1, 0)])
    core = lax.axis_index("core").reshape(1)
    met_normed = lax.optimization_barrier(rms_normed(met_inputs, norm_gain))
    values = times_weights(core, both, other, met_normed, pieces, 0, ahead_rows)
    values, met_residual = lax.optimization_barrier((values, met_residual))
    activated, gelu_back = jax.vjp(gelu_tanh, values[:, :share])
    up_value = values[:, share : 2 * share]
    hidden = (activated * up_value).astype(jnp.bfloat16)
    back_hidden = times_weights(
        core, both, other, met_residual, pieces, pieces * ahead_rows, back_rows
    )[:, :share]
    back_gate = gelu_back(back_hidden * up_value)[0].astype(jnp.bfloat16)
    back_up = (back_hidden * activated).astype(jnp.bfloat16)

    def blank(rows):
        return jnp.zeros((param_count, rows, token_count), jnp.bfloat16)

    lead = 2 * share - (height - back_rows)
    by_plane = (z_count, core_count, slice_rows, token_count)
    deltas = make_deltas(
        jnp.concatenate([back_gate, back_up, blank(ahead_rows - 2 * share)], axis=1),
        jnp.concatenate([blank(lead), hidden, blank(back_rows - share - lead)], axis=1),
        met_normed.reshape(by_plane),
        met_residual.reshape(by_plane),
        height,
    )
    owned = exchange(deltas, ("core",) + XY)

    gram = pair_products(owned, core_count * param_count)
    gram = jnp.sum(exchange(gram, ("core",) + XY), axis=0)
    gram = exchange(jnp.broadcast_to(gram[None], (z_count,) + gram.shape), "z")
    order = neighbours.reshape(z_count, core_count).T.reshape(1, -1)
    update, relative = finish(gram, order, owned, z_count)
    update = exchange(update, "z").astype(jnp.float32)

    def placed(index):
        rows = update[:, index * share : (index + 1) * share]
        return rows.reshape(hidden_units, slice_rows).T

    return (
        placed(0),
        placed(1),
        placed(2),
        relative.reshape(core_count, z_count).T.reshape(-1),
    )


def solution(mesh):
    torus = Mesh(mesh.devices.reshape(16, 2, 4, 4), ("z", "core", "x", "y"))
    in_specs = (
        P(ZC, None, XY),
        P(ZC, None, XY),
        P(),
        P(None, XY),
        P(None, XY),
        P(XY, None),
        P(),
    )
    out_specs = (P(ZC, XY), P(ZC, XY), P(ZC, XY), P())
    return jax.shard_map(
        on_device, mesh=torus, in_specs=in_specs, out_specs=out_specs, check_vma=False
    )
```
